128 devices in a mesh: grp: 8 (over y, core), tok: 16 (over x, z).
Axes of the slice: x: 4, y: 4, z: 4, core: 2. Of those that a mesh axis runs over, the one named last changes fastest.
Arguments:
- tokens: bfloat16 [8, 2048, 1280], P('grp', 'tok'), may hold values from -6 to 6
- seg_lengths: int32 [8, 32], P('grp'), may hold values from 1 to 256, 2048 in all within a row
- prefix_keys: bfloat16 [8, 4096, 1280], P('grp', 'tok'), may hold values from -6 to 6
- prefix_values: bfloat16 [8, 4096, 1280], P('grp', 'tok'), may hold values from -0.4375 to 0.4375
- w_qkv: bfloat16 [1280, 3840], replicated, may hold values from -0.15625 to 0.15625
- w_out: bfloat16 [1280, 1280], replicated, may hold values from -0.15625 to 0.15625
- qk_scale: float32 [1280], replicated, may hold values from 0.3 to 10
- attn_rate: float32 [1280], replicated, may hold values from 0.05 to 0.5
- w_up: bfloat16 [1280, 5120], P(None, 'grp'), may hold values from -0.15625 to 0.15625
- w_gate: bfloat16 [1280, 5120], P(None, 'grp'), may hold values from -0.15625 to 0.15625
- w_down: bfloat16 [5120, 1280], P('grp'), may hold values from -0.078125 to 0.078125
- up_scale: float32 [5120], P('grp'), may hold values from 0.5 to 2
- gate_scale: float32 [5120], P('grp'), may hold values from 0.5 to 2
- mlp_rate: float32 [1280], replicated, may hold values from 0.05 to 0.5
Outputs:
- mixed: bfloat16 [8, 2048, 1280], P('grp', 'tok')
The draws below stay inside these ranges and needn't reach their ends.
Inputs may be any that keep to these rules, and one draw needn't show every extreme that they name: `seg_lengths`: row g lists the lengths of group g's 32 requests in order of position; they sum to 2048 and the longest is exactly 256.
All inputs are finite; a program needn't handle non-finite values.
Results may differ from the reference program's by a relative error of at most 0.0085.
The reference program's roundings to bfloat16 on the way count: a program that leaves them out, or rounds other values in their place, can miss the bound.
Values may be sent and summed in bfloat16 or wider, within the bound.
A program may use at most 128 MiB of HBM per device.

```python
import math
import jax
import jax.numpy as jnp
import numpy as np
from jax import lax

D = 1280
HEADS = 20
HEAD = 64
FF = 5120
TOK_DEV = 128
PREFIX_DEV = 256
SUFFIX = 2048
PREFIX = 4096
REQS = 32
N_GRP = 8
N_TOK = 16


def draw_qk_scale(key, part):
    scales = jnp.exp(jax.random.uniform(jax.random.fold_in(key, 5), (D,), minval=math.log(0.3), maxval=math.log(3.0)))
    scales = jnp.clip(scales, 0.3, 3.0)
    return scales.astype(jnp.float32)


def draw_prefix_keys(key, part):
    result = jnp.clip(jax.random.normal(jax.random.fold_in(key, 8), (N_GRP, PREFIX, D)), -6.0, 6.0)
    return result.astype(jnp.bfloat16)


def block_levels(own_key, extent, cuts, low, high):
    gain = 1.0
    for axis_at, blocks in cuts:
        draws = jax.random.uniform(jax.random.fold_in(jax.random.fold_in(own_key, 6), axis_at), (blocks,), jnp.float32, low / len(cuts), high / len(cuts))
        gain = gain * jnp.repeat(jnp.exp(draws), extent[axis_at] // blocks).reshape((-1,) + (1,) * (len(extent) - 1 - axis_at))
    return gain


def split_up(amount, total, bound, skew):
    portions = [(1 << 20) // math.isqrt(rank ** skew) + 1 for rank in range(2, amount + 1)]
    spare, counts = total - bound - (amount - 1), [1] * (amount - 1)
    while spare > 0:
        free = [i for i in range(amount - 1) if counts[i] < bound]
        whole, budget = sum([portions[i] for i in free]), spare
        for i in free:
            more = min(bound - counts[i], max(1, budget * portions[i] // whole), spare)
            counts[i] = counts[i] + more
            spare = spare - more
    return np.array([bound] + counts)


def uneven(rng, number_of, total, bound, slope):
    if number_of == 2:
        one = jax.random.randint(rng, (), max(1, total - bound), min(bound, total - 1) + 1)
        return jnp.stack([one, total - one])
    sizes = jnp.asarray(split_up(number_of, total, bound, slope), jnp.int32)
    couples = (number_of - 1) // 2
    source_of, sink = sizes[1:1 + 2 * couples:2], sizes[2:2 + 2 * couples:2]
    slack = jnp.minimum(source_of - 1, bound - sink)
    passed = jax.random.randint(jax.random.fold_in(rng, 1), (couples,), 0, 1 << 20) % (slack + 1)
    sizes = sizes.at[1:1 + 2 * couples:2].set(source_of - passed).at[2:2 + 2 * couples:2].set(sink + passed)
    return sizes[jax.random.permutation(jax.random.fold_in(rng, 2), number_of)]


def noise(key, extent, width, bound, shards=(), kind=jnp.bfloat16):
    array = jax.random.normal(key, extent, jnp.float32) * width
    if len(shards) > 0:
        array = block_levels(key, extent, shards, -0.22, 0.18) * array
    return jnp.clip(array, min=-bound, max=bound).astype(kind)


def setup_inputs(seed: int = 0) -> dict:
    key_of = jax.random.split(jax.random.key(seed), 15)
    return {
        "tokens": noise(key_of[0], (N_GRP, SUFFIX, D), 1.0, 6.0, ((0, 8), (1, 16))),
        "seg_lengths": jax.vmap(lambda own: uneven(own, REQS, SUFFIX, 2 * TOK_DEV, 2))(jax.random.split(key_of[1], N_GRP)).reshape((N_GRP, REQS)).astype(jnp.int32),
        "prefix_keys": draw_prefix_keys(jax.random.fold_in(key_of[14], 71), 0),
        "prefix_values": noise(key_of[3], (N_GRP, PREFIX, D), (D ** -0.5), 0.4375, ((0, 8), (1, 16))),
        "w_qkv": noise(key_of[4], (D, 3 * D), D ** -0.5, 0.15625),
        "w_out": noise(key_of[5], (D, D), D ** -0.5, 0.15625),
        "qk_scale": draw_qk_scale(jax.random.fold_in(key_of[14], 71), 0),
        "attn_rate": jnp.clip(jnp.exp(jax.random.uniform(key_of[7], (D,), jnp.float32, math.log(0.05), math.log(0.5))), 0.05, 0.5),
        "w_up": noise(key_of[8], (D, FF), D ** -0.5, 0.15625, ((1, 8),)),
        "w_gate": noise(key_of[9], (D, FF), D ** -0.5, 0.15625, ((1, 8),)),
        "w_down": noise(key_of[10], (FF, D), FF ** -0.5, 0.078125, ((0, 8),)),
        "up_scale": jnp.clip(jnp.exp(math.log(2.0) - 1.3862944 * jax.random.uniform(key_of[11], (FF,), jnp.float32) ** block_levels(key_of[11], (FF,), ((0, 8),), -0.2, 0.2)), 0.5, 2.0),
        "gate_scale": jnp.clip(jnp.exp(math.log(2.0) - 1.3862944 * jax.random.uniform(key_of[12], (FF,), jnp.float32) ** block_levels(key_of[12], (FF,), ((0, 8),), -0.2, 0.2)), 0.5, 2.0),
        "mlp_rate": jnp.clip(jnp.exp(jax.random.uniform(key_of[13], (D,), jnp.float32, math.log(0.05), math.log(0.5))), 0.05, 0.5),
    }


EPS = 1e-06

def unit(vector):
    return vector * lax.rsqrt(lax.optimization_barrier(jnp.sum(vector * vector, axis=-1, keepdims=True)) + EPS)

def head_unit(vector, scaling):
    per_head = vector.reshape(vector.shape[0], HEADS, HEAD)
    return unit(per_head) * scaling.reshape(HEADS, HEAD)

def segment_of(position, lengths):
    bounds = jnp.cumsum(lengths, dtype=jnp.int32)
    return lax.optimization_barrier(jnp.sum((position[:, None] >= bounds[None, :]).astype(jnp.int32), axis=1)).astype(jnp.int32)

def block_state(query, keys, values, allowed):
    scores = math.sqrt(HEAD) * jnp.einsum('rhd,khd->rhk', query.astype(jnp.float32), keys.astype(jnp.float32))
    if allowed is not None:
        scores = jnp.where(allowed[:, None, :], scores, -jnp.inf)
    maximum = lax.optimization_barrier(jnp.max(scores, axis=-1))
    weights = jnp.exp(scores - maximum[..., None])
    totals = lax.optimization_barrier(jnp.sum(weights, axis=-1))
    rounded = lax.optimization_barrier(weights.astype(jnp.bfloat16))
    blended = jnp.einsum('rhk,khd->rhd', rounded.astype(jnp.float32), values.astype(jnp.float32))
    return ((blended / totals[..., None]).astype(jnp.bfloat16), maximum, totals)

def start_state(block):
    blended, maximum, totals = block
    return (maximum, totals, totals[..., None] * blended.astype(jnp.float32))

def merge_block(running, block):
    maximum, totals, accum = running
    blended, block_max, block_sum = block
    new_max = jnp.maximum(maximum, block_max)
    shrink_old = jnp.exp(maximum - new_max)
    weight_new = jnp.exp(block_max - new_max) * block_sum
    return (new_max, totals * shrink_old + weight_new, accum * shrink_old[..., None] + weight_new[..., None] * blended.astype(jnp.float32))

def one_group(tokens, lengths, prefix_keys, prefix_values, w_qkv, w_out, qk_scale, attn_rate, w_up, w_gate, w_down, up_scale, gate_scale, mlp_rate):
    hidden_state = unit(tokens.astype(jnp.float32))
    projected = jnp.dot(hidden_state.astype(jnp.bfloat16), w_qkv, preferred_element_type=jnp.float32)
    query = head_unit(projected[:, :D], qk_scale).astype(jnp.bfloat16)
    suffix_keys = head_unit(projected[:, D:2 * D], qk_scale).astype(jnp.bfloat16)
    suffix_values = projected[:, 2 * D:].astype(jnp.bfloat16).reshape(SUFFIX, HEADS, HEAD)
    cached_keys = head_unit(prefix_keys.astype(jnp.float32), qk_scale).astype(jnp.bfloat16)
    cached_values = prefix_values.reshape(PREFIX, HEADS, HEAD)
    position = jnp.arange(SUFFIX, dtype=jnp.int32)
    segment = segment_of(position, lengths)
    margin = 2 * TOK_DEV
    keys_pad = jnp.concatenate([jnp.zeros((margin, HEADS, HEAD), jnp.bfloat16), suffix_keys], axis=0)
    values_pad = jnp.concatenate([jnp.zeros((margin, HEADS, HEAD), jnp.bfloat16), suffix_values], axis=0)
    pos_pad = jnp.concatenate([jnp.arange(-margin, 0, dtype=jnp.int32), position])
    seg_pad = jnp.concatenate([jnp.full((margin,), -1, jnp.int32), segment])

    def local_block(block_index):
        begin = (block_index * TOK_DEV).astype(jnp.int32)
        query_rows = lax.dynamic_slice_in_dim(query, begin, TOK_DEV, 0)
        key_rows = lax.dynamic_slice_in_dim(keys_pad, begin, 3 * TOK_DEV, 0)
        value_rows = lax.dynamic_slice_in_dim(values_pad, begin, 3 * TOK_DEV, 0)
        key_pos = lax.dynamic_slice_in_dim(pos_pad, begin, 3 * TOK_DEV, 0)
        key_seg = lax.dynamic_slice_in_dim(seg_pad, begin, 3 * TOK_DEV, 0)
        query_pos = lax.dynamic_slice_in_dim(position, begin, TOK_DEV, 0)
        query_seg = lax.dynamic_slice_in_dim(segment, begin, TOK_DEV, 0)
        allowed = (key_seg[None, :] == query_seg[:, None]) & (key_pos[None, :] <= query_pos[:, None]) & (key_pos[None, :] >= 0)
        return block_state(query_rows, key_rows, value_rows, allowed)
    local = lax.map(local_block, jnp.arange(N_TOK, dtype=jnp.int32))
    local = (local[0].reshape(SUFFIX, HEADS, HEAD), local[1].reshape(SUFFIX, HEADS), local[2].reshape(SUFFIX, HEADS))
    shard_keys = cached_keys.reshape(N_TOK, PREFIX_DEV, HEADS, HEAD)
    shard_values = cached_values.reshape(N_TOK, PREFIX_DEV, HEADS, HEAD)

    def add_shard(running, matched):
        return (merge_block(running, block_state(query, matched[0], matched[1], None)), None)
    final, ignored = lax.scan(add_shard, start_state(local), (shard_keys, shard_values))
    maximum, totals, accum = final
    attn_mix = (accum / totals[..., None]).astype(jnp.bfloat16).reshape(SUFFIX, D)
    attended = unit(jnp.dot(attn_mix, w_out, preferred_element_type=jnp.float32))
    hidden_state = unit(hidden_state + attn_rate * (attended - hidden_state))
    flattened = hidden_state.astype(jnp.bfloat16)
    up_part = jnp.dot(flattened, w_up, preferred_element_type=jnp.float32) * up_scale
    gate_part = jnp.dot(flattened, w_gate, preferred_element_type=jnp.float32) * (gate_scale * math.sqrt(D))
    act = (up_part * jax.nn.silu(gate_part)).astype(jnp.bfloat16)
    mlp_dir = unit(jnp.dot(act, w_down, preferred_element_type=jnp.float32))
    hidden_state = unit(hidden_state + mlp_rate * (mlp_dir - hidden_state))
    return (math.sqrt(D) * hidden_state).astype(jnp.bfloat16)

def reference(tokens, seg_lengths, prefix_keys, prefix_values, w_qkv, w_out, qk_scale, attn_rate, w_up, w_gate, w_down, up_scale, gate_scale, mlp_rate):

    def one_pass(group_items):
        return one_group(group_items[0], group_items[1], group_items[2], group_items[3], w_qkv, w_out, qk_scale, attn_rate, w_up, w_gate, w_down, up_scale, gate_scale, mlp_rate)
    return lax.map(one_pass, (tokens, seg_lengths, prefix_keys, prefix_values))
```

```python
import functools
import math

import jax
import jax.numpy as jnp
from jax import lax
from jax.experimental import pallas as pl
from jax.experimental.pallas import tpu as pltpu
from jax.sharding import PartitionSpec as P

D = 1280
HEADS = 20
HEAD = 64
LOCAL_HEADS = 5
HROWS = 320
ROWS = 128
PREF = 256
EPS = 1e-06
MESH = pl.DeviceIdType.MESH
F32 = jnp.float32
BF16 = jnp.bfloat16


def unit(vector):
    return vector * lax.rsqrt(jnp.sum(vector * vector, axis=-1, keepdims=True) + EPS)


def head_unit_t(cols, scaling):
    per_head = cols.reshape(HEADS, HEAD, cols.shape[1])
    norm = lax.rsqrt(jnp.sum(per_head * per_head, axis=1, keepdims=True) + EPS)
    return (per_head * norm) * scaling.reshape(HEADS, HEAD, 1)


def attn_kernel(
    qkv_ref, pre_ref, start_ref, out_ref,
    qs, kv, qz, kt, skt, part, stat, ret, rstat, merged, att,
    qs_s, qs_r, kv_s, kv_r, qz_s, qz_r, ret_s, ret_r, rst_s, rst_r, att_s, att_r, loc,
):
    tok = lax.axis_index("tok")
    x, z = tok // 4, tok % 4

    def at_x(i):
        return {"tok": ((x + i) % 4) * 4 + z}

    def at_z(i):
        return {"tok": x * 4 + (z + i) % 4}

    def remote(src, dst, send, recv, dev):
        return pltpu.make_async_remote_copy(
            src_ref=src, dst_ref=dst, send_sem=send, recv_sem=recv, device_id=dev, device_id_type=MESH
        )

    barrier = pltpu.get_barrier_semaphore()
    for i in (1, 2, 3):
        pl.semaphore_signal(barrier, inc=1, device_id=at_x(i), device_id_type=MESH)
        pl.semaphore_signal(barrier, inc=1, device_id=at_z(i), device_id_type=MESH)
    pl.semaphore_wait(barrier, 6)

    sends = []

    own_q = pltpu.make_async_copy(qkv_ref.at[:, x], qs.at[0], loc.at[0])
    own_q.start()
    own_p = pltpu.make_async_copy(pre_ref.at[:, x], kv.at[0], loc.at[1])
    own_p.start()
    for i in (2, 1, 3):
        c = remote(qkv_ref.at[:, (x + i) % 4], qs.at[4 - i], qs_s.at[i - 1], qs_r.at[3 - i], at_x(i))
        c.start()
        sends.append(c)
    for i in (2, 1, 3):
        c = remote(pre_ref.at[:, (x + i) % 4], kv.at[4 - i], kv_s.at[i - 1], kv_r.at[3 - i], at_x(i))
        c.start()
        sends.append(c)

    def forward_q(j):
        for e in (2, 1, 3):
            c = remote(
                qs.at[j, 0], qz.at[(4 - e) - 1, j], qz_s.at[e - 1, j], qz_r.at[(4 - e) - 1, j], at_z(e)
            )
            c.start()
            sends.append(c)

    own_q.wait()
    forward_q(0)
    for j in (1, 3, 2):
        remote(qs.at[j], qs.at[j], qs_s.at[j - 1], qs_r.at[j - 1], at_x(0)).wait_recv()
        forward_q(j)

    own_p.wait()
    for j in (0, 1, 3, 2):
        if j > 0:
            remote(kv.at[j], kv.at[j], kv_s.at[j - 1], kv_r.at[j - 1], at_x(0)).wait_recv()
        for h in range(LOCAL_HEADS):
            rows = pl.ds(h * HEAD, HEAD)
            kt[h, pl.ds(j * PREF, PREF), :] = kv[j, 0, rows, :].T
            skt[j, h] = qs[j, 1, rows, :].T

    for d in range(4):
        for j in range(4):
            stat[d, j] = jnp.zeros((8, ROWS), F32)

    def tile(e, j0, wrapped):
        xq = [(x + j0 + a) % 4 for a in (0, 1)]
        for h in range(LOCAL_HEADS):
            rows = pl.ds(h * HEAD, HEAD)
            qh = [qs[j0 + a, 0, rows, :] if e == 0 else qz[e - 1, j0 + a, rows, :] for a in (0, 1)]
            s = jnp.dot(kt[h], jnp.concatenate(qh, axis=1), preferred_element_type=F32)
            m = jnp.max(s, axis=0, keepdims=True)
            if e < 3:
                loc_s, slots = [], []
                for a in (0, 1):
                    slot = (j0 + a + 4 - wrapped) % 4
                    slots.append(slot)
                    zq = (z + e) % 4
                    tq = xq[a] * 4 + zq
                    t = jnp.dot(skt[slot, h], qh[a], preferred_element_type=F32)
                    kpos = (tq - e) * ROWS + lax.broadcasted_iota(jnp.int32, (ROWS, ROWS), 0)
                    qpos = tq * ROWS + lax.broadcasted_iota(jnp.int32, (ROWS, ROWS), 1)
                    first = start_ref[tq, pl.ds(0, 1), :]
                    allowed = (kpos >= first) & (kpos <= qpos)
                    loc_s.append(jnp.where(allowed, t, -1e30))
                ls = jnp.concatenate(loc_s, axis=1)
                m = jnp.maximum(m, jnp.max(ls, axis=0, keepdims=True))
            p = jnp.exp(s - m)
            total = jnp.sum(p, axis=0, keepdims=True)
            pb = p.astype(BF16)
            o = jnp.zeros((HEAD, 2 * ROWS), F32)
            for j in range(4):
                o += jnp.dot(kv[j, 1, rows, :], pb[j * PREF : (j + 1) * PREF, :], preferred_element_type=F32)
            if e < 3:
                lp = jnp.exp(ls - m)
                total += jnp.sum(lp, axis=0, keepdims=True)
                lpb = lp.astype(BF16)
                lo = [
                    jnp.dot(qs[slots[a], 2, rows, :], lpb[:, a * ROWS : (a + 1) * ROWS], preferred_element_type=F32)
                    for a in (0, 1)
                ]
                o += jnp.concatenate(lo, axis=1)
            o = (o / total).astype(BF16)
            lse = m + jnp.log(total)
            for a in (0, 1):
                part[e, j0 + a, rows, :] = o[:, a * ROWS : (a + 1) * ROWS]
                stat[e, j0 + a, pl.ds(h, 1), :] = lse[:, a * ROWS : (a + 1) * ROWS]

    for e in (0, 1, 3, 2):
        wrapped = (z + e) // 4
        if e > 0:
            for j in range(4):
                remote(qz.at[e - 1, j], qz.at[e - 1, j], qz_s.at[e - 1, j], qz_r.at[e - 1, j], at_z(0)).wait_recv()
        for j0 in (0, 2):
            tile(e, j0, wrapped)
            if e > 0:
                for j in (j0, j0 + 1):
                    back = (4 - e) - 1
                    c = remote(part.at[e, j], ret.at[back, j], ret_s.at[e - 1, j], ret_r.at[back, j], at_z(e))
                    c.start()
                    sends.append(c)
                    c = remote(stat.at[e, j], rstat.at[back, j], rst_s.at[e - 1, j], rst_r.at[back, j], at_z(e))
                    c.start()
                    sends.append(c)

    for j in (2, 1, 3, 0):
        for b in range(3):
            remote(ret.at[b, j], ret.at[b, j], ret_s.at[b, j], ret_r.at[b, j], at_z(0)).wait_recv()
            remote(rstat.at[b, j], rstat.at[b, j], rst_s.at[b, j], rst_r.at[b, j], at_z(0)).wait_recv()
        lses = [stat[0, j]] + [rstat[b, j] for b in range(3)]
        top = functools.reduce(jnp.maximum, lses)
        weights = [jnp.exp(v - top) for v in lses]
        inverse = 1.0 / sum(weights[1:], weights[0])
        coefs = [w * inverse for w in weights]
        for h in range(LOCAL_HEADS):
            rows = pl.ds(h * HEAD, HEAD)
            acc = coefs[0][h : h + 1, :] * part[0, j, rows, :].astype(F32)
            for b in range(3):
                acc += coefs[b + 1][h : h + 1, :] * ret[b, j, rows, :].astype(F32)
            merged[j, rows, :] = acc.astype(BF16)
        if j > 0:
            c = remote(merged.at[j], att.at[4 - j], att_s.at[j - 1], att_r.at[3 - j], at_x(j))
            c.start()
            sends.append(c)

    out_ref[x] = merged[0]
    for j in (1, 3, 2):
        remote(att.at[j], att.at[j], att_s.at[j - 1], att_r.at[j - 1], at_x(0)).wait_recv()
        out_ref[(x + j) % 4] = att[j]
    for c in sends:
        c.wait_send()


def attention(qkv, pre, start):
    dma = pltpu.SemaphoreType.DMA
    vmem = pl.BlockSpec(memory_space=pltpu.VMEM)
    return pl.pallas_call(
        attn_kernel,
        out_shape=jax.ShapeDtypeStruct((4, HROWS, ROWS), BF16),
        in_specs=[vmem] * 3,
        out_specs=vmem,
        scratch_shapes=[
            pltpu.VMEM((4, 3, HROWS, ROWS), BF16),
            pltpu.VMEM((4, 2, HROWS, PREF), BF16),
            pltpu.VMEM((3, 4, HROWS, ROWS), BF16),
            pltpu.VMEM((LOCAL_HEADS, 4 * PREF, HEAD), BF16),
            pltpu.VMEM((4, LOCAL_HEADS, ROWS, HEAD), BF16),
            pltpu.VMEM((4, 4, HROWS, ROWS), BF16),
            pltpu.VMEM((4, 4, 8, ROWS), F32),
            pltpu.VMEM((3, 4, HROWS, ROWS), BF16),
            pltpu.VMEM((3, 4, 8, ROWS), F32),
            pltpu.VMEM((4, HROWS, ROWS), BF16),
            pltpu.VMEM((4, HROWS, ROWS), BF16),
            dma((3,)), dma((3,)), dma((3,)), dma((3,)),
            dma((3, 4)), dma((3, 4)), dma((3, 4)), dma((3, 4)), dma((3, 4)), dma((3, 4)),
            dma((3,)), dma((3,)), dma((2,)),
        ],
        compiler_params=pltpu.CompilerParams(
            collective_id=0, has_side_effects=True, vmem_limit_bytes=48 * 1024 * 1024
        ),
        name="attn",
    )(qkv, pre, start)


def segment_start(lengths):
    ends = jnp.cumsum(lengths, dtype=jnp.int32)
    position = jnp.arange(16 * ROWS, dtype=jnp.int32)
    return jnp.max(jnp.where(ends[None, :] <= position[:, None], ends[None, :], 0), axis=1)


def body(
    tokens, seg_lengths, prefix_keys, prefix_values, w_qkv, w_out, qk_scale, attn_rate,
    w_up, w_gate, w_down, up_scale, gate_scale, mlp_rate,
):
    hidden_state = unit(tokens[0].astype(F32))
    proj = lax.dot_general(
        w_qkv, hidden_state.astype(BF16), (((0,), (1,)), ((), ())), preferred_element_type=F32
    )
    query = (head_unit_t(proj[:D], qk_scale).astype(BF16) * BF16(math.sqrt(HEAD))).reshape(4, HROWS, ROWS)
    skeys = head_unit_t(proj[D : 2 * D], qk_scale).astype(BF16).reshape(4, HROWS, ROWS)
    svals = proj[2 * D :].astype(BF16).reshape(4, HROWS, ROWS)
    ckeys = head_unit_t(prefix_keys[0].astype(F32).T, qk_scale).astype(BF16).reshape(4, HROWS, PREF)
    cvals = prefix_values[0].T.reshape(4, HROWS, PREF)
    start = segment_start(seg_lengths[0]).reshape(16, 1, ROWS)
    start = jnp.broadcast_to(start, (16, 8, ROWS))
    att = attention(jnp.stack([query, skeys, svals]), jnp.stack([ckeys, cvals]), start)
    attn_mix = att.reshape(D, ROWS)
    attended = unit(lax.dot_general(attn_mix, w_out, (((0,), (0,)), ((), ())), preferred_element_type=F32))
    hidden_state = unit(hidden_state + attn_rate * (attended - hidden_state))
    flattened = hidden_state.astype(BF16)
    piece = lax.all_gather(flattened, "grp", axis=0, tiled=True)
    up_part = jnp.dot(piece, w_up, preferred_element_type=F32) * up_scale
    gate_part = jnp.dot(piece, w_gate, preferred_element_type=F32) * (gate_scale * math.sqrt(D))
    act = (up_part * jax.nn.silu(gate_part)).astype(BF16)
    partials = jnp.dot(act, w_down, preferred_element_type=F32)
    summed = lax.psum_scatter(partials.astype(BF16), "grp", scatter_dimension=0, tiled=True).astype(F32)
    mlp_dir = unit(summed)
    hidden_state = unit(hidden_state + mlp_rate * (mlp_dir - hidden_state))
    return (math.sqrt(D) * hidden_state).astype(BF16)[None]


def solution(mesh):
    in_specs = (
        P("grp", "tok", None), P("grp", None), P("grp", "tok", None), P("grp", "tok", None),
        P(), P(), P(), P(), P(None, "grp"), P(None, "grp"), P("grp", None), P("grp"), P("grp"), P(),
    )
    return jax.shard_map(body, mesh=mesh, in_specs=in_specs, out_specs=P("grp", "tok", None), check_vma=False)
```

```python
import functools
import math

import jax
import jax.numpy as jnp
from jax import lax
from jax.experimental import pallas as pl
from jax.experimental.pallas import tpu as pltpu
from jax.sharding import PartitionSpec as P

D = 1280
HEADS = 20
HEAD = 64
LOCAL_HEADS = 5
HROWS = 320
ROWS = 128
PREF = 256
EPS = 1e-06
MESH = pl.DeviceIdType.MESH
F32 = jnp.float32
BF16 = jnp.bfloat16


def unit(vector):
    return vector * lax.rsqrt(jnp.sum(vector * vector, axis=-1, keepdims=True) + EPS)


def head_unit_t(cols, scaling):
    per_head = cols.reshape(HEADS, HEAD, cols.shape[1])
    norm = lax.rsqrt(jnp.sum(per_head * per_head, axis=1, keepdims=True) + EPS)
    return (per_head * norm) * scaling.reshape(HEADS, HEAD, 1)


def attn_kernel(
    qkv_ref, pre_ref, start_ref, out_ref,
    qs, kv, qz, kt, skt, part, stat, ret, rstat, merged, att,
    qs_s, qs_r, kv_s, kv_r, qz_s, qz_r, ret_s, ret_r, rst_s, rst_r, att_s, att_r, loc,
):
    tok = lax.axis_index("tok")
    x, z = tok // 4, tok % 4

    def at_x(i):
        return {"tok": ((x + i) % 4) * 4 + z}

    def at_z(i):
        return {"tok": x * 4 + (z + i) % 4}

    def remote(src, dst, send, recv, dev):
        return pltpu.make_async_remote_copy(
            src_ref=src, dst_ref=dst, send_sem=send, recv_sem=recv, device_id=dev, device_id_type=MESH
        )

    barrier = pltpu.get_barrier_semaphore()
    for i in (1, 2, 3):
        pl.semaphore_signal(barrier, inc=1, device_id=at_x(i), device_id_type=MESH)
        pl.semaphore_signal(barrier, inc=1, device_id=at_z(i), device_id_type=MESH)
    pl.semaphore_wait(barrier, 6)

    sends = []

    own_q = pltpu.make_async_copy(qkv_ref.at[:, x], qs.at[0], loc.at[0])
    own_q.start()
    own_p = pltpu.make_async_copy(pre_ref.at[:, x], kv.at[0], loc.at[1])
    own_p.start()
    for i in (2, 1, 3):
        c = remote(qkv_ref.at[:, (x + i) % 4], qs.at[4 - i], qs_s.at[i - 1], qs_r.at[3 - i], at_x(i))
        c.start()
        sends.append(c)
    for i in (2, 1, 3):
        c = remote(pre_ref.at[:, (x + i) % 4], kv.at[4 - i], kv_s.at[i - 1], kv_r.at[3 - i], at_x(i))
        c.start()
        sends.append(c)

    def forward_q(j):
        for e in (2, 1, 3):
            c = remote(
                qs.at[j, 0], qz.at[(4 - e) - 1, j], qz_s.at[e - 1, j], qz_r.at[(4 - e) - 1, j], at_z(e)
            )
            c.start()
            sends.append(c)

    own_q.wait()
    forward_q(0)
    for j in (1, 3, 2):
        remote(qs.at[j], qs.at[j], qs_s.at[j - 1], qs_r.at[j - 1], at_x(0)).wait_recv()
        forward_q(j)

    own_p.wait()
    for j in (0, 1, 3, 2):
        if j > 0:
            remote(kv.at[j], kv.at[j], kv_s.at[j - 1], kv_r.at[j - 1], at_x(0)).wait_recv()
        for h in range(LOCAL_HEADS):
            rows = pl.ds(h * HEAD, HEAD)
            kt[h, pl.ds(j * PREF, PREF), :] = kv[j, 0, rows, :].T
            skt[j, h] = qs[j, 1, rows, :].T

    for d in range(4):
        for j in range(4):
            stat[d, j] = jnp.zeros((8, ROWS), F32)

    def tile(e, j0, wrapped):
        xq = [(x + j0 + a) % 4 for a in (0, 1)]
        for h in range(LOCAL_HEADS):
            rows = pl.ds(h * HEAD, HEAD)
            qh = [qs[j0 + a, 0, rows, :] if e == 0 else qz[e - 1, j0 + a, rows, :] for a in (0, 1)]
            s = jnp.dot(kt[h], jnp.concatenate(qh, axis=1), preferred_element_type=F32)
            m = jnp.max(s, axis=0, keepdims=True)
            if e < 3:
                loc_s, slots = [], []
                for a in (0, 1):
                    slot = (j0 + a + 4 - wrapped) % 4
                    slots.append(slot)
                    zq = (z + e) % 4
                    tq = xq[a] * 4 + zq
                    t = jnp.dot(skt[slot, h], qh[a], preferred_element_type=F32)
                    kpos = (tq - e) * ROWS + lax.broadcasted_iota(jnp.int32, (ROWS, ROWS), 0)
                    qpos = tq * ROWS + lax.broadcasted_iota(jnp.int32, (ROWS, ROWS), 1)
                    first = start_ref[tq, pl.ds(0, 1), :]
                    allowed = (kpos >= first) & (kpos <= qpos)
                    loc_s.append(jnp.where(allowed, t, -1e30))
                ls = jnp.concatenate(loc_s, axis=1)
                m = jnp.maximum(m, jnp.max(ls, axis=0, keepdims=True))
            p = jnp.exp(s - m)
            total = jnp.sum(p, axis=0, keepdims=True)
            pb = p.astype(BF16)
            o = jnp.zeros((HEAD, 2 * ROWS), F32)
            for j in range(4):
                o += jnp.dot(kv[j, 1, rows, :], pb[j * PREF : (j + 1) * PREF, :], preferred_element_type=F32)
            if e < 3:
                lp = jnp.exp(ls - m)
                total += jnp.sum(lp, axis=0, keepdims=True)
                lpb = lp.astype(BF16)
                lo = [
                    jnp.dot(qs[slots[a], 2, rows, :], lpb[:, a * ROWS : (a + 1) * ROWS], preferred_element_type=F32)
                    for a in (0, 1)
                ]
                o += jnp.concatenate(lo, axis=1)
            o = (o / total).astype(BF16)
            lse = m + jnp.log(total)
            for a in (0, 1):
                part[e, j0 + a, rows, :] = o[:, a * ROWS : (a + 1) * ROWS]
                stat[e, j0 + a, pl.ds(h, 1), :] = lse[:, a * ROWS : (a + 1) * ROWS]

    for e in (0, 1, 3, 2):
        wrapped = (z + e) // 4
        if e > 0:
            for j in range(4):
                remote(qz.at[e - 1, j], qz.at[e - 1, j], qz_s.at[e - 1, j], qz_r.at[e - 1, j], at_z(0)).wait_recv()
        for j0 in (0, 2):
            tile(e, j0, wrapped)
            if e > 0:
                for j in (j0, j0 + 1):
                    back = (4 - e) - 1
                    c = remote(part.at[e, j], ret.at[back, j], ret_s.at[e - 1, j], ret_r.at[back, j], at_z(e))
                    c.start()
                    sends.append(c)
                    c = remote(stat.at[e, j], rstat.at[back, j], rst_s.at[e - 1, j], rst_r.at[back, j], at_z(e))
                    c.start()
                    sends.append(c)

    for j in (2, 1, 3, 0):
        for b in range(3):
            remote(ret.at[b, j], ret.at[b, j], ret_s.at[b, j], ret_r.at[b, j], at_z(0)).wait_recv()
            remote(rstat.at[b, j], rstat.at[b, j], rst_s.at[b, j], rst_r.at[b, j], at_z(0)).wait_recv()
        lses = [stat[0, j]] + [rstat[b, j] for b in range(3)]
        top = functools.reduce(jnp.maximum, lses)
        weights = [jnp.exp(v - top) for v in lses]
        inverse = 1.0 / sum(weights[1:], weights[0])
        coefs = [w * inverse for w in weights]
        for h in range(LOCAL_HEADS):
            rows = pl.ds(h * HEAD, HEAD)
            acc = coefs[0][h : h + 1, :] * part[0, j, rows, :].astype(F32)
            for b in range(3):
                acc += coefs[b + 1][h : h + 1, :] * ret[b, j, rows, :].astype(F32)
            merged[j, rows, :] = acc.astype(BF16)
        if j > 0:
            c = remote(merged.at[j], att.at[4 - j], att_s.at[j - 1], att_r.at[3 - j], at_x(j))
            c.start()
            sends.append(c)

    out_ref[x] = merged[0]
    for j in (1, 3, 2):
        remote(att.at[j], att.at[j], att_s.at[j - 1], att_r.at[j - 1], at_x(0)).wait_recv()
        out_ref[(x + j) % 4] = att[j]
    for c in sends:
        c.wait_send()


def attention(qkv, pre, start):
    dma = pltpu.SemaphoreType.DMA
    vmem = pl.BlockSpec(memory_space=pltpu.VMEM)
    return pl.pallas_call(
        attn_kernel,
        out_shape=jax.ShapeDtypeStruct((4, HROWS, ROWS), BF16),
        in_specs=[vmem] * 3,
        out_specs=vmem,
        scratch_shapes=[
            pltpu.VMEM((4, 3, HROWS, ROWS), BF16),
            pltpu.VMEM((4, 2, HROWS, PREF), BF16),
            pltpu.VMEM((3, 4, HROWS, ROWS), BF16),
            pltpu.VMEM((LOCAL_HEADS, 4 * PREF, HEAD), BF16),
            pltpu.VMEM((4, LOCAL_HEADS, ROWS, HEAD), BF16),
            pltpu.VMEM((4, 4, HROWS, ROWS), BF16),
            pltpu.VMEM((4, 4, 8, ROWS), F32),
            pltpu.VMEM((3, 4, HROWS, ROWS), BF16),
            pltpu.VMEM((3, 4, 8, ROWS), F32),
            pltpu.VMEM((4, HROWS, ROWS), BF16),
            pltpu.VMEM((4, HROWS, ROWS), BF16),
            dma((3,)), dma((3,)), dma((3,)), dma((3,)),
            dma((3, 4)), dma((3, 4)), dma((3, 4)), dma((3, 4)), dma((3, 4)), dma((3, 4)),
            dma((3,)), dma((3,)), dma((2,)),
        ],
        compiler_params=pltpu.CompilerParams(
            collective_id=0, has_side_effects=True, vmem_limit_bytes=48 * 1024 * 1024
        ),
        name="attn",
    )(qkv, pre, start)


def mlp_kernel(
    att_ref, tok_ref, wout_hbm, arate_ref, wup_hbm, wgate_hbm, wdown_hbm, uscale_ref, gscale_ref, mrate_ref, out_ref,
    wout, wup, wgate, wdown, hid, blocks, give, take, total, send_y, recv_y,
    w_sem, gs, gr, fs, fr, cs, cr, xs, xr, ys, yr,
):
    grp = lax.axis_index("grp")
    y, c = grp // 2, grp % 2

    def at_y(i):
        return {"grp": ((y + i) % 4) * 2 + c}

    partner = {"grp": y * 2 + (1 - c)}

    def remote(src, dst, send, recv, dev):
        return pltpu.make_async_remote_copy(
            src_ref=src, dst_ref=dst, send_sem=send, recv_sem=recv, device_id=dev, device_id_type=MESH
        )

    loads = []
    for n, (src, dst) in enumerate(((wout_hbm, wout), (wup_hbm, wup), (wgate_hbm, wgate), (wdown_hbm, wdown))):
        load = pltpu.make_async_copy(src, dst, w_sem.at[n])
        load.start()
        loads.append(load)

    barrier = pltpu.get_barrier_semaphore()
    for i in (1, 2, 3):
        pl.semaphore_signal(barrier, inc=1, device_id=at_y(i), device_id_type=MESH)
    pl.semaphore_signal(barrier, inc=1, device_id=partner, device_id_type=MESH)
    pl.semaphore_wait(barrier, 4)

    hidden = unit(tok_ref[...].astype(F32))
    loads[0].wait()
    mix = att_ref[...].T
    attended = unit(jnp.dot(mix, wout[...], preferred_element_type=F32))
    hidden = unit(hidden + arate_ref[...] * (attended - hidden))
    hid[...] = hidden
    top = pl.ds(0, ROWS)
    bot = pl.ds(ROWS, ROWS)
    blocks[0, top, :] = hidden.astype(BF16)

    sends = []

    def start(copy):
        copy.start()
        sends.append(copy)

    start(remote(blocks.at[0, top], blocks.at[3, top], gs.at[0], gr.at[0], at_y(1)))
    start(remote(blocks.at[0, top], blocks.at[1, top], gs.at[1], gr.at[1], at_y(3)))
    start(remote(blocks.at[0, top], blocks.at[0, bot], cs.at[0], cr.at[0], partner))
    halves = (pl.ds(0, 64), pl.ds(64, 64))
    mirror = (pl.ds(ROWS, 64), pl.ds(ROWS + 64, 64))

    def wait_block(i, rows, sem):
        ref = blocks.at[i, rows]
        remote(ref, ref, gs.at[0], sem, partner).wait_recv()

    def swiglu(i, n):
        a = blocks[i]
        up = jnp.dot(a, wup[...], preferred_element_type=F32) * uscale_ref[...]
        gate = jnp.dot(a, wgate[...], preferred_element_type=F32) * gscale_ref[...]
        act = (up * (gate / (1.0 + jnp.exp(-gate)))).astype(BF16)
        both = jnp.dot(act, wdown[...], preferred_element_type=F32)
        give[n] = both[ROWS:].astype(BF16)
        total[n] = both[:ROWS]
        start(remote(give.at[n], take.at[n], xs.at[n], xr.at[n], partner))

    def join(i, n):
        ref = take.at[n]
        remote(ref, ref, xs.at[n], xr.at[n], partner).wait_recv()
        both = total[n] + take[n].astype(F32)
        if i == 0:
            total[n] = both
        else:
            send_y[n - 1] = both.astype(BF16)
            start(remote(send_y.at[n - 1], recv_y.at[n - 1], ys.at[n - 1], yr.at[n - 1], at_y(i)))

    for load in loads[1:]:
        load.wait()
    wait_block(0, bot, cr.at[0])
    swiglu(0, 0)
    wait_block(3, top, gr.at[0])
    start(remote(blocks.at[3, halves[0]], blocks.at[2, halves[0]], fs.at[0], fr.at[0], at_y(1)))
    start(remote(blocks.at[3, top], blocks.at[3, bot], cs.at[1], cr.at[1], partner))
    wait_block(1, top, gr.at[1])
    start(remote(blocks.at[1, halves[1]], blocks.at[2, halves[1]], fs.at[1], fr.at[1], at_y(3)))
    start(remote(blocks.at[1, top], blocks.at[1, bot], cs.at[2], cr.at[2], partner))
    wait_block(3, bot, cr.at[1])
    swiglu(3, 1)
    for k in (0, 1):
        wait_block(2, halves[k], fr.at[k])
        start(remote(blocks.at[2, halves[k]], blocks.at[2, mirror[k]], cs.at[3 + k], cr.at[3 + k], partner))
    wait_block(1, bot, cr.at[2])
    join(3, 1)
    swiglu(1, 2)
    for k in (0, 1):
        wait_block(2, mirror[k], cr.at[3 + k])
    join(1, 2)
    swiglu(2, 3)
    join(2, 3)
    join(0, 0)
    summed = total[0]
    for n in (0, 1, 2):
        ref = recv_y.at[n]
        remote(ref, ref, ys.at[n], yr.at[n], partner).wait_recv()
        summed += recv_y[n].astype(F32)
    hidden = hid[...]
    hidden = unit(hidden + mrate_ref[...] * (unit(summed) - hidden))
    out_ref[...] = (math.sqrt(D) * hidden).astype(BF16)
    for copy in sends:
        copy.wait_send()


def mlp(att, tokens, w_out, attn_rate, w_up, w_gate, w_down, up_scale, gate_scale, mlp_rate):
    dma = pltpu.SemaphoreType.DMA
    vmem = pl.BlockSpec(memory_space=pltpu.VMEM)
    anyw = pl.BlockSpec(memory_space=pl.ANY)
    ff = w_up.shape[1]
    return pl.pallas_call(
        mlp_kernel,
        out_shape=jax.ShapeDtypeStruct((ROWS, D), BF16),
        in_specs=[vmem, vmem, anyw, vmem, anyw, anyw, anyw, vmem, vmem, vmem],
        out_specs=vmem,
        scratch_shapes=[
            pltpu.VMEM((D, D), BF16),
            pltpu.VMEM((D, ff), BF16),
            pltpu.VMEM((D, ff), BF16),
            pltpu.VMEM((ff, D), BF16),
            pltpu.VMEM((ROWS, D), F32),
            pltpu.VMEM((4, 2 * ROWS, D), BF16),
            pltpu.VMEM((4, ROWS, D), BF16),
            pltpu.VMEM((4, ROWS, D), BF16),
            pltpu.VMEM((4, ROWS, D), F32),
            pltpu.VMEM((3, ROWS, D), BF16),
            pltpu.VMEM((3, ROWS, D), BF16),
            dma((4,)), dma((2,)), dma((2,)), dma((2,)), dma((2,)), dma((5,)), dma((5,)),
            dma((4,)), dma((4,)), dma((3,)), dma((3,)),
        ],
        compiler_params=pltpu.CompilerParams(
            collective_id=1, has_side_effects=True, vmem_limit_bytes=48 * 1024 * 1024
        ),
        name="mlp",
    )(
        att, tokens, w_out, attn_rate.reshape(1, D), w_up, w_gate, w_down,
        up_scale.reshape(1, ff), gate_scale.reshape(1, ff) * math.sqrt(D), mlp_rate.reshape(1, D),
    )


def segment_start(lengths):
    ends = jnp.cumsum(lengths, dtype=jnp.int32)
    position = jnp.arange(16 * ROWS, dtype=jnp.int32)
    return jnp.max(jnp.where(ends[None, :] <= position[:, None], ends[None, :], 0), axis=1)


def body(
    tokens, seg_lengths, prefix_keys, prefix_values, w_qkv, w_out, qk_scale, attn_rate,
    w_up, w_gate, w_down, up_scale, gate_scale, mlp_rate,
):
    hidden_state = unit(tokens[0].astype(F32))
    proj = lax.dot_general(
        w_qkv, hidden_state.astype(BF16), (((0,), (1,)), ((), ())), preferred_element_type=F32
    )
    query = (head_unit_t(proj[:D], qk_scale).astype(BF16) * BF16(math.sqrt(HEAD))).reshape(4, HROWS, ROWS)
    skeys = head_unit_t(proj[D : 2 * D], qk_scale).astype(BF16).reshape(4, HROWS, ROWS)
    svals = proj[2 * D :].astype(BF16).reshape(4, HROWS, ROWS)
    ckeys = head_unit_t(prefix_keys[0].astype(F32).T, qk_scale).astype(BF16).reshape(4, HROWS, PREF)
    cvals = prefix_values[0].T.reshape(4, HROWS, PREF)
    start = segment_start(seg_lengths[0]).reshape(16, 1, ROWS)
    start = jnp.broadcast_to(start, (16, 8, ROWS))
    att = attention(jnp.stack([query, skeys, svals]), jnp.stack([ckeys, cvals]), start)
    out = mlp(
        att.reshape(D, ROWS), tokens[0], w_out, attn_rate, w_up, w_gate, w_down, up_scale, gate_scale, mlp_rate
    )
    return out[None]


def solution(mesh):
    in_specs = (
        P("grp", "tok", None), P("grp", None), P("grp", "tok", None), P("grp", "tok", None),
        P(), P(), P(), P(), P(None, "grp"), P(None, "grp"), P("grp", None), P("grp"), P("grp"), P(),
    )
    return jax.shard_map(body, mesh=mesh, in_specs=in_specs, out_specs=P("grp", "tok", None), check_vma=False)
```

```python
import functools
import math

import jax
import jax.numpy as jnp
from jax import lax
from jax.experimental import pallas as pl
from jax.experimental.pallas import tpu as pltpu
from jax.sharding import PartitionSpec as P

D = 1280
HEAD = 64
LOCAL_HEADS = 5
HROWS = 320
ROWS = 128
PREF = 256
REQS = 32
EPS = 1e-06
MESH = pl.DeviceIdType.MESH
F32 = jnp.float32
BF16 = jnp.bfloat16


def unit(vector):
    return vector * lax.rsqrt(jnp.sum(vector * vector, axis=-1, keepdims=True) + EPS)


def head_unit(cols, scale):
    per_head = cols.reshape(2, HEAD, cols.shape[1])
    norm = lax.rsqrt(jnp.sum(per_head * per_head, axis=1, keepdims=True) + EPS)
    return (per_head * norm).reshape(cols.shape) * scale


def layer_kernel(
    lengths_ref, tok_ref, pk_ref, pv_ref, wqkv_hbm, wout_hbm, scale_ref, arate_ref, wup_hbm, wgate_hbm, wdown_hbm,
    uscale_ref, gscale_ref, mrate_ref, out_ref,
    wqkv, wout, wup, wgate, wdown, scale_t,
    key_s, val_s, q_s, sk_s, kx, vx, qx, sx, qz, kt, skt, starts, mask, sbuf, kloc, vloc, part, stat, ret, rstat, merged, att, mix_t,
    hid, blocks, give, take, total, send_y, recv_y, w_sem, sem,
):
    tok, grp = lax.axis_index("tok"), lax.axis_index("grp")
    x, z = tok // 4, tok % 4
    y, c = grp // 2, grp % 2

    def at_x(i):
        return {"tok": ((x + i) % 4) * 4 + z}

    def at_z(i):
        return {"tok": x * 4 + (z + i) % 4}

    def at_y(i):
        return {"grp": ((y + i) % 4) * 2 + c}

    partner = {"grp": y * 2 + (1 - c)}
    used = [0]
    arrivals = {}
    sends = []

    def send(name, src, dst, dev):
        n = used[0]
        used[0] += 2
        copy = pltpu.make_async_remote_copy(
            src_ref=src, dst_ref=dst, send_sem=sem.at[n], recv_sem=sem.at[n + 1], device_id=dev, device_id_type=MESH
        )
        copy.start()
        sends.append(copy)
        assert name not in arrivals
        arrivals[name] = (dst, n)

    def arrive(name):
        dst, n = arrivals[name]
        pltpu.make_async_remote_copy(
            src_ref=dst, dst_ref=dst, send_sem=sem.at[n], recv_sem=sem.at[n + 1], device_id=partner,
            device_id_type=MESH,
        ).wait_recv()

    barrier = pltpu.get_barrier_semaphore()
    for i in (1, 2, 3):
        for dev in (at_x(i), at_z(i), at_y(i)):
            pl.semaphore_signal(barrier, inc=1, device_id=dev, device_id_type=MESH)
    pl.semaphore_signal(barrier, inc=1, device_id=partner, device_id_type=MESH)

    loads = []

    def load(src, dst):
        copy = pltpu.make_async_copy(src, dst, w_sem.at[len(loads)])
        copy.start()
        loads.append(copy)

    for n in range(3):
        cols = pl.ds(n * D, D)
        load(wqkv_hbm.at[:, cols], wqkv.at[:, cols])
    load(wout_hbm, wout)
    load(wup_hbm, wup)
    load(wgate_hbm, wgate)
    load(wdown_hbm, wdown)

    for b in range(10):
        lanes = pl.ds(b * 128, 128)
        scale_t[lanes, :] = jnp.broadcast_to(scale_ref[:, lanes], (128, 128)).T
    for b in range(10):
        lanes = pl.ds(b * 128, 128)
        scale = scale_t[lanes, :]
        cols = pk_ref[:, lanes].astype(F32).T
        key_s[lanes, :] = head_unit(cols, jnp.concatenate([scale, scale], axis=1)).astype(BF16)
    pl.semaphore_wait(barrier, 10)

    def rows_of(ref, i):
        return ref.at[pl.ds(((x + i) % 4) * HROWS, HROWS), :]

    for i in (2, 1, 3):
        send(("k", 4 - i), rows_of(key_s, i), kx.at[4 - i], at_x(i))

    for b in range(10):
        lanes = pl.ds(b * 128, 128)
        val_s[lanes, :] = pv_ref[:, lanes].T

    hidden = unit(tok_ref[...].astype(F32))
    hid[...] = hidden
    hidden = hidden.astype(BF16)

    def project(n, b):
        cols = jnp.dot(hidden, wqkv[:, n * D + b * 256 : n * D + b * 256 + 256], preferred_element_type=F32)
        return [cols[:, a * 128 : a * 128 + 128].T for a in (0, 1)]

    loads[0].wait()
    for b in range(5):
        for a, cols in enumerate(project(0, b)):
            lanes = pl.ds(b * 256 + a * 128, 128)
            query = head_unit(cols, scale_t[lanes, :]).astype(BF16)
            q_s[lanes, :] = query * BF16(math.sqrt(HEAD))
    for i in (2, 1, 3):
        send(("q", 4 - i), rows_of(q_s, i), qx.at[4 - i], at_x(i))
    qx[0] = q_s[pl.ds(pl.multiple_of(x * HROWS, HROWS), HROWS), :]

    def forward_q(j):
        for e in (2, 1, 3):
            send(("qz", 4 - e, j), qx.at[j], qz.at[(4 - e) - 1, j], at_z(e))

    forward_q(0)
    for i in (2, 1, 3):
        send(("v", 4 - i), rows_of(val_s, i), vx.at[4 - i], at_x(i))
    for n in (1, 2):
        loads[n].wait()
        for b in range(5):
            for a, cols in enumerate(project(n, b)):
                lanes = pl.ds(b * 256 + a * 128, 128)
                if n == 1:
                    cols = head_unit(cols, scale_t[lanes, :])
                sk_s[n - 1, lanes, :] = cols.astype(BF16)
    for i in (2, 1, 3):
        src = sk_s.at[:, pl.ds(((x + i) % 4) * HROWS, HROWS), :]
        send(("s", 4 - i), src, sx.at[4 - i], at_x(i))
    own = pl.ds(pl.multiple_of(x * HROWS, HROWS), HROWS)
    kx[0] = key_s[own, :]
    vx[0] = val_s[own, :]
    sx[0] = sk_s[:, own, :]

    position = (
        lax.broadcasted_iota(jnp.int32, (16, ROWS), 0) * ROWS + lax.broadcasted_iota(jnp.int32, (16, ROWS), 1)
    )
    end = jnp.int32(0)
    first = jnp.zeros((16, ROWS), jnp.int32)
    for r in range(REQS):
        end = end + lengths_ref[0, r]
        first = jnp.where(position >= end, end, first)
    for t in range(16):
        starts[t] = jnp.broadcast_to(first[t : t + 1, :], (8, ROWS))
    for e in range(3):
        for j in range(4):
            tq = ((x + j) % 4) * 4 + (z + e) % 4
            kpos = (tq - e) * ROWS + lax.broadcasted_iota(jnp.int32, (ROWS, ROWS), 0)
            qpos = tq * ROWS + lax.broadcasted_iota(jnp.int32, (ROWS, ROWS), 1)
            allowed = (kpos >= starts[tq, pl.ds(0, 1), :]) & (kpos <= qpos)
            bias = jnp.where(allowed, 0.0, -1e30)
            apart = jnp.full((ROWS, ROWS), -1e30, F32)
            mask[e, j // 2, pl.ds((j % 2) * ROWS, ROWS), :] = jnp.concatenate(
                [apart, bias] if j % 2 else [bias, apart], axis=1
            )
    for d in range(4):
        for j in range(4):
            stat[d, j] = jnp.zeros((8, ROWS), F32)

    def turn_keys(j):
        for h in range(LOCAL_HEADS):
            kt[h, pl.ds(j * PREF, PREF), :] = kx[j, pl.ds(h * HEAD, HEAD), :].T

    turn_keys(0)
    for j in (1, 3, 2):
        arrive(("k", j))
        turn_keys(j)
    for j in (1, 3, 2):
        arrive(("q", j))
        forward_q(j)
    for j in (1, 3, 2):
        arrive(("v", j))

    def fold(v):
        return v.reshape(v.shape[0] // 8, 8, v.shape[1])

    def attend(e):
        local = e < 3

        def head_rows(h):
            return pl.ds(pl.multiple_of(h * HEAD, HEAD), HEAD)

        def score(h, n, j, high):
            j0, rows = 2 * n, head_rows(h)
            q = [qx[j0 + a, rows, :] if e == 0 else qz[e - 1, j0 + a, rows, :] for a in (0, 1)]
            keys = kt[h, pl.ds(j * PREF, PREF), :] if j < 4 else kloc[e, n, h]
            s = jnp.dot(keys, jnp.concatenate(q, axis=1), preferred_element_type=F32)
            if j == 4:
                s = s + mask[e, n]
            sbuf[n, pl.ds(j * PREF, PREF), :] = s
            top = jnp.max(fold(s), axis=0)
            return top if high is None else jnp.maximum(high, top)

        def blend(h, n, j, m, added, o):
            rows = head_rows(h)
            p = jnp.exp(sbuf[n, pl.ds(j * PREF, PREF), :] - m)
            more = jnp.sum(fold(p), axis=0)
            values = vx[j, rows, :] if j < 4 else vloc[e, n, rows, :]
            t = jnp.dot(values, p.astype(BF16), preferred_element_type=F32)
            return (more, t) if o is None else (added + more, o + t)

        parts = 5 if local else 4

        def step(h, n, high, after):
            m = jnp.max(high, axis=0, keepdims=True)
            high, added, o = None, None, None
            for j in range(parts):
                high = score(after, 1 - n, j, high)
                added, o = blend(h, n, j, m, added, o)
            added = jnp.sum(added, axis=0, keepdims=True)
            o = (o * (1.0 / added)).astype(BF16)
            lse = m + jnp.log(added)
            for a in (0, 1):
                lanes = slice(a * ROWS, (a + 1) * ROWS)
                part[e, 2 * n + a, head_rows(h), :] = o[:, lanes]
                stat[e, 2 * n + a, pl.ds(h, 1), :] = lse[:, lanes]
            return high

        def both_tiles(h, high):
            high = step(h, 0, high, h)
            return step(h, 1, high, jnp.minimum(h + 1, LOCAL_HEADS - 1))

        high = None
        for j in range(parts):
            high = score(0, 0, j, high)
        lax.fori_loop(0, LOCAL_HEADS, both_tiles, high)
        if e > 0:
            for j in range(4):
                send(("o", 4 - e, j), part.at[e, j], ret.at[(4 - e) - 1, j], at_z(e))
                send(("l", 4 - e, j), stat.at[e, j], rstat.at[(4 - e) - 1, j], at_z(e))

    for e in (3, 2, 1, 0):
        if e > 0:
            for j in range(4):
                arrive(("qz", e, j))
        attend(e)
        if e == 3:
            for j in range(4):
                if j > 0:
                    arrive(("s", j))
                for h in range(LOCAL_HEADS):
                    skt[j, h] = sx[j, 0, pl.ds(h * HEAD, HEAD), :].T
            for d in range(3):
                for j in range(4):
                    slot = (j + 4 - (z + d) // 4) % 4
                    half = pl.ds((j % 2) * ROWS, ROWS)
                    for h in range(LOCAL_HEADS):
                        kloc[d, j // 2, h, half, :] = skt[slot, h]
                    vloc[d, j // 2, :, half] = sx[slot, 1]

    for j in (2, 1, 3, 0):
        for b in (1, 2, 3):
            arrive(("o", b, j))
            arrive(("l", b, j))
        lses = [stat[0, j]] + [rstat[b, j] for b in range(3)]
        top = functools.reduce(jnp.maximum, lses)
        weights = [jnp.exp(v - top) for v in lses]
        inverse = 1.0 / sum(weights[1:], weights[0])
        coefs = [w * inverse for w in weights]
        for h in range(LOCAL_HEADS):
            rows = pl.ds(h * HEAD, HEAD)
            acc = coefs[0][h : h + 1, :] * part[0, j, rows, :].astype(F32)
            for b in range(3):
                acc += coefs[b + 1][h : h + 1, :] * ret[b, j, rows, :].astype(F32)
            merged[j, rows, :] = acc.astype(BF16)
        if j > 0:
            send(("a", 4 - j), merged.at[j], att.at[4 - j], at_x(j))
    mix_t[own, :] = merged[0]
    for j in (2, 1, 3):
        arrive(("a", j))
        mix_t[pl.ds(pl.multiple_of(((x + j) % 4) * HROWS, HROWS), HROWS), :] = att[j]

    loads[3].wait()
    mix = jnp.concatenate([mix_t[pl.ds(b * 128, 128), :].T for b in range(10)], axis=1)
    attended = unit(jnp.dot(mix, wout[...], preferred_element_type=F32))
    hidden = hid[...]
    hidden = unit(hidden + arate_ref[...] * (attended - hidden))
    hid[...] = hidden
    upper, lower = pl.ds(0, ROWS), pl.ds(ROWS, ROWS)
    blocks[0, upper, :] = hidden.astype(BF16)

    halves = (pl.ds(0, 64), pl.ds(64, 64))
    mirror = (pl.ds(ROWS, 64), pl.ds(ROWS + 64, 64))
    send(("b", 3), blocks.at[0, upper], blocks.at[3, upper], at_y(1))
    send(("b", 1), blocks.at[0, upper], blocks.at[1, upper], at_y(3))
    send(("p", 0), blocks.at[0, upper], blocks.at[0, lower], partner)

    def swiglu(i):
        a = blocks[i]
        up = jnp.dot(a, wup[...], preferred_element_type=F32) * uscale_ref[...]
        gate = jnp.dot(a, wgate[...], preferred_element_type=F32) * (gscale_ref[...] * math.sqrt(D))
        act = (up * (gate / (1.0 + jnp.exp(-gate)))).astype(BF16)
        both = jnp.dot(act, wdown[...], preferred_element_type=F32)
        give[i] = both[ROWS:].astype(BF16)
        total[i] = both[:ROWS]
        send(("x", i), give.at[i], take.at[i], partner)

    def join(i):
        arrive(("x", i))
        both = total[i] + take[i].astype(F32)
        if i == 0:
            total[0] = both
        else:
            send_y[i - 1] = both.astype(BF16)
            send(("y", 4 - i), send_y.at[i - 1], recv_y.at[3 - i], at_y(i))

    for n in (4, 5, 6):
        loads[n].wait()
    arrive(("p", 0))
    swiglu(0)
    arrive(("b", 3))
    send(("f", 0), blocks.at[3, halves[0]], blocks.at[2, halves[0]], at_y(1))
    send(("p", 3), blocks.at[3, upper], blocks.at[3, lower], partner)
    arrive(("b", 1))
    send(("f", 1), blocks.at[1, halves[1]], blocks.at[2, halves[1]], at_y(3))
    send(("p", 1), blocks.at[1, upper], blocks.at[1, lower], partner)
    arrive(("p", 3))
    swiglu(3)
    for k in (0, 1):
        arrive(("f", k))
        send(("g", k), blocks.at[2, halves[k]], blocks.at[2, mirror[k]], partner)
    arrive(("p", 1))
    join(3)
    swiglu(1)
    for k in (0, 1):
        arrive(("g", k))
    join(1)
    swiglu(2)
    join(2)
    join(0)
    summed = total[0]
    for i in (1, 3, 2):
        arrive(("y", i))
        summed += recv_y[i - 1].astype(F32)
    hidden = hid[...]
    hidden = unit(hidden + mrate_ref[...] * (unit(summed) - hidden))
    out_ref[...] = (math.sqrt(D) * hidden).astype(BF16)
    for copy in sends:
        copy.wait_send()


def body(
    tokens, seg_lengths, prefix_keys, prefix_values, w_qkv, w_out, qk_scale, attn_rate,
    w_up, w_gate, w_down, up_scale, gate_scale, mlp_rate,
):
    vmem = pl.BlockSpec(memory_space=pltpu.VMEM)
    smem = pl.BlockSpec(memory_space=pltpu.SMEM)
    hbm = pl.BlockSpec(memory_space=pltpu.HBM)
    ff = w_up.shape[1]
    vm = pltpu.VMEM
    out = pl.pallas_call(
        layer_kernel,
        out_shape=jax.ShapeDtypeStruct((ROWS, D), BF16),
        in_specs=[smem, vmem, vmem, vmem, hbm, hbm, vmem, vmem, hbm, hbm, hbm, vmem, vmem, vmem],
        out_specs=vmem,
        scratch_shapes=[
            vm((D, 3 * D), BF16), vm((D, D), BF16), vm((D, ff), BF16), vm((D, ff), BF16), vm((ff, D), BF16),
            vm((D, 128), F32),
            vm((D, PREF), BF16), vm((D, PREF), BF16), vm((D, ROWS), BF16), vm((2, D, ROWS), BF16),
            vm((4, HROWS, PREF), BF16), vm((4, HROWS, PREF), BF16), vm((4, HROWS, ROWS), BF16),
            vm((4, 2, HROWS, ROWS), BF16), vm((3, 4, HROWS, ROWS), BF16),
            vm((LOCAL_HEADS, 4 * PREF, HEAD), BF16), vm((4, LOCAL_HEADS, ROWS, HEAD), BF16),
            vm((16, 8, ROWS), jnp.int32), vm((3, 2, PREF, PREF), F32), vm((2, 5 * PREF, 2 * ROWS), F32),
            vm((3, 2, LOCAL_HEADS, PREF, HEAD), BF16), vm((3, 2, HROWS, PREF), BF16),
            vm((4, 4, HROWS, ROWS), BF16), vm((4, 4, 8, ROWS), F32),
            vm((3, 4, HROWS, ROWS), BF16), vm((3, 4, 8, ROWS), F32),
            vm((4, HROWS, ROWS), BF16), vm((4, HROWS, ROWS), BF16), vm((D, ROWS), BF16),
            vm((ROWS, D), F32), vm((4, 2 * ROWS, D), BF16), vm((4, ROWS, D), BF16), vm((4, ROWS, D), BF16),
            vm((4, ROWS, D), F32), vm((3, ROWS, D), BF16), vm((3, ROWS, D), BF16),
            pltpu.SemaphoreType.DMA((7,)), pltpu.SemaphoreType.DMA((140,)),
        ],
        compiler_params=pltpu.CompilerParams(
            collective_id=0, has_side_effects=True, vmem_limit_bytes=56 * 1024 * 1024
        ),
        name="layer",
    )(
        seg_lengths, tokens[0], prefix_keys[0], prefix_values[0], w_qkv, w_out, qk_scale.reshape(1, D),
        attn_rate.reshape(1, D), w_up, w_gate, w_down, up_scale.reshape(1, ff), gate_scale.reshape(1, ff),
        mlp_rate.reshape(1, D),
    )
    return out[None]


def solution(mesh):
    in_specs = (
        P("grp", "tok", None), P("grp", None), P("grp", "tok", None), P("grp", "tok", None),
        P(), P(), P(), P(), P(None, "grp"), P(None, "grp"), P("grp", None), P("grp"), P("grp"), P(),
    )
    return jax.shard_map(body, mesh=mesh, in_specs=in_specs, out_specs=P("grp", "tok", None), check_vma=False)
```

```python
import functools
import math

import jax
import jax.numpy as jnp
from jax import lax
from jax.experimental import pallas as pl
from jax.experimental.pallas import tpu as pltpu
from jax.sharding import PartitionSpec as P

D = 1280
HEAD = 64
LOCAL_HEADS = 5
HROWS = 320
ROWS = 128
PREF = 256
REQS = 32
EPS = 1e-06
MESH = pl.DeviceIdType.MESH
F32 = jnp.float32
BF16 = jnp.bfloat16


def unit(vector):
    return vector * lax.rsqrt(jnp.sum(vector * vector, axis=-1, keepdims=True) + EPS)


def head_unit(cols, scale):
    per_head = cols.reshape(2, HEAD, cols.shape[1])
    norm = lax.rsqrt(jnp.sum(per_head * per_head, axis=1, keepdims=True) + EPS)
    return (per_head * norm).reshape(cols.shape) * scale


def layer_kernel(
    lengths_ref, tok_hbm, pk_hbm, pv_hbm, wqkv_hbm, wout_hbm, scale_ref, arate_ref, wup_hbm, wgate_hbm, wdown_hbm,
    uscale_ref, gscale_ref, mrate_ref, out_ref,
    tok_ref, pk_ref, pv_ref, wqkv, wout, wup, wgate, wdown, scale_t,
    key_s, val_s, q_s, sk_s, kx, vx, qx, sx, qz, kt, skt, starts, mask, sbuf, kloc, vloc, held, tops, sums, part, stat, ret, rstat, merged, att, mix_t,
    hid, blocks, give, take, total, send_y, recv_y, w_sem, sem,
):
    tok, grp = lax.axis_index("tok"), lax.axis_index("grp")
    x, z = tok // 4, tok % 4
    y, c = grp // 2, grp % 2

    def at_x(i):
        return {"tok": ((x + i) % 4) * 4 + z}

    def at_z(i):
        return {"tok": x * 4 + (z + i) % 4}

    def at_y(i):
        return {"grp": ((y + i) % 4) * 2 + c}

    partner = {"grp": y * 2 + (1 - c)}
    used = [0]
    arrivals = {}
    sends = []

    def send(name, src, dst, dev):
        n = used[0]
        used[0] += 2
        copy = pltpu.make_async_remote_copy(
            src_ref=src, dst_ref=dst, send_sem=sem.at[n], recv_sem=sem.at[n + 1], device_id=dev, device_id_type=MESH
        )
        copy.start()
        sends.append(copy)
        assert name not in arrivals
        arrivals[name] = (dst, n)

    def arrive(name):
        dst, n = arrivals[name]
        pltpu.make_async_remote_copy(
            src_ref=dst, dst_ref=dst, send_sem=sem.at[n], recv_sem=sem.at[n + 1], device_id=partner,
            device_id_type=MESH,
        ).wait_recv()

    loads = {}

    def load(name, src, dst):
        copy = pltpu.make_async_copy(src, dst, w_sem.at[len(loads)])
        copy.start()
        loads[name] = copy

    load("pk", pk_hbm, pk_ref)
    load("tok", tok_hbm, tok_ref)
    load("pv", pv_hbm, pv_ref)
    barrier = pltpu.get_barrier_semaphore()
    for i in (1, 2, 3):
        for dev in (at_x(i), at_z(i), at_y(i)):
            pl.semaphore_signal(barrier, inc=1, device_id=dev, device_id_type=MESH)
    pl.semaphore_signal(barrier, inc=1, device_id=partner, device_id_type=MESH)
    for n in range(3):
        cols = pl.ds(n * D, D)
        load(n, wqkv_hbm.at[:, cols], wqkv.at[:, cols])
    load("out", wout_hbm, wout)
    load("up", wup_hbm, wup)
    load("gate", wgate_hbm, wgate)
    load("down", wdown_hbm, wdown)

    for b in range(10):
        lanes = pl.ds(b * 128, 128)
        scale_t[lanes, :] = jnp.broadcast_to(scale_ref[lanes].reshape(1, 128), (128, 128)).T
    loads["pk"].wait()
    for b in range(10):
        lanes = pl.ds(b * 128, 128)
        scale = scale_t[lanes, :]
        cols = pk_ref[:, lanes].astype(F32).T
        key_s[lanes, :] = head_unit(cols, jnp.concatenate([scale, scale], axis=1)).astype(BF16)
    pl.semaphore_wait(barrier, 10)

    def rows_of(ref, i):
        return ref.at[pl.ds(((x + i) % 4) * HROWS, HROWS), :]

    for i in (1, 3):
        send(("k", 4 - i), rows_of(key_s, i), kx.at[4 - i], at_x(i))

    loads["pv"].wait()
    for b in range(10):
        lanes = pl.ds(b * 128, 128)
        val_s[lanes, :] = pv_ref[:, lanes].T

    loads["tok"].wait()
    hidden = unit(tok_ref[...].astype(F32))
    hid[...] = hidden
    hidden = hidden.astype(BF16)

    def project(n, b):
        cols = jnp.dot(hidden, wqkv[:, n * D + b * 256 : n * D + b * 256 + 256], preferred_element_type=F32)
        return [cols[:, a * 128 : a * 128 + 128].T for a in (0, 1)]

    loads[0].wait()
    for b in range(5):
        for a, cols in enumerate(project(0, b)):
            lanes = pl.ds(b * 256 + a * 128, 128)
            query = head_unit(cols, scale_t[lanes, :]).astype(BF16)
            q_s[lanes, :] = query * BF16(math.sqrt(HEAD))
    for i in (2, 1, 3):
        send(("q", 4 - i), rows_of(q_s, i), qx.at[4 - i], at_x(i))
    qx[0] = q_s[pl.ds(pl.multiple_of(x * HROWS, HROWS), HROWS), :]

    def forward_q(j):
        for e in (2, 1, 3):
            send(("qz", 4 - e, j), qx.at[j], qz.at[(4 - e) - 1, j], at_z(e))

    forward_q(0)
    for i in (1, 3):
        send(("v", 4 - i), rows_of(val_s, i), vx.at[4 - i], at_x(i))
    send(("k", 2), rows_of(key_s, 2), kx.at[2], at_x(2))
    send(("v", 2), rows_of(val_s, 2), vx.at[2], at_x(2))
    for n in (1, 2):
        loads[n].wait()
        for b in range(5):
            for a, cols in enumerate(project(n, b)):
                lanes = pl.ds(b * 256 + a * 128, 128)
                if n == 1:
                    cols = head_unit(cols, scale_t[lanes, :])
                sk_s[n - 1, lanes, :] = cols.astype(BF16)
    for i in (2, 1, 3):
        src = sk_s.at[:, pl.ds(((x + i) % 4) * HROWS, HROWS), :]
        send(("s", 4 - i), src, sx.at[4 - i], at_x(i))
    own = pl.ds(pl.multiple_of(x * HROWS, HROWS), HROWS)
    kx[0] = key_s[own, :]
    vx[0] = val_s[own, :]
    sx[0] = sk_s[:, own, :]

    position = (
        lax.broadcasted_iota(jnp.int32, (16, ROWS), 0) * ROWS + lax.broadcasted_iota(jnp.int32, (16, ROWS), 1)
    )
    end = jnp.int32(0)
    first = jnp.zeros((16, ROWS), jnp.int32)
    for r in range(REQS):
        end = end + lengths_ref[0, r]
        first = jnp.where(position >= end, end, first)
    for t in range(16):
        starts[t] = jnp.broadcast_to(first[t : t + 1, :], (8, ROWS))
    for e in range(3):
        for j in range(4):
            tq = ((x + j) % 4) * 4 + (z + e) % 4
            kpos = (tq - e) * ROWS + lax.broadcasted_iota(jnp.int32, (ROWS, ROWS), 0)
            qpos = tq * ROWS + lax.broadcasted_iota(jnp.int32, (ROWS, ROWS), 1)
            allowed = (kpos >= starts[tq, pl.ds(0, 1), :]) & (kpos <= qpos)
            bias = jnp.where(allowed, 0.0, -1e30)
            apart = jnp.full((ROWS, ROWS), -1e30, F32)
            mask[e, j // 2, pl.ds((j % 2) * ROWS, ROWS), :] = jnp.concatenate(
                [apart, bias] if j % 2 else [bias, apart], axis=1
            )
    for d in range(4):
        for j in range(4):
            stat[d, j] = jnp.zeros((8, ROWS), F32)

    def turn_keys(j):
        for h in range(LOCAL_HEADS):
            kt[h, pl.ds(j * PREF, PREF), :] = kx[j, pl.ds(h * HEAD, HEAD), :].T

    turn_keys(0)
    for j in (1, 3):
        arrive(("k", j))
        turn_keys(j)
    for j in (1, 3, 2):
        arrive(("q", j))
        forward_q(j)
    for j in (1, 3):
        arrive(("v", j))

    def fold(v):
        return v.reshape(v.shape[0] // 8, 8, v.shape[1])

    def attend(e, parts, last):
        def head_rows(h):
            return pl.ds(pl.multiple_of(h * HEAD, HEAD), HEAD)

        def score(h, n, j, high):
            j0, rows = 2 * n, head_rows(h)
            q = [qx[j0 + a, rows, :] if e == 0 else qz[e - 1, j0 + a, rows, :] for a in (0, 1)]
            keys = kt[h, pl.ds(j * PREF, PREF), :] if j < 4 else kloc[e, n, h]
            s = jnp.dot(keys, jnp.concatenate(q, axis=1), preferred_element_type=F32)
            if j == 4:
                s = s + mask[e, n]
            sbuf[n, pl.ds(j * PREF, PREF), :] = s
            top = jnp.max(fold(s), axis=0)
            return top if high is None else jnp.maximum(high, top)

        def blend(h, n, j, m, added, o):
            rows = head_rows(h)
            p = jnp.exp(sbuf[n, pl.ds(j * PREF, PREF), :] - m)
            more = jnp.sum(fold(p), axis=0)
            values = vx[j, rows, :] if j < 4 else vloc[e, n, rows, :]
            t = jnp.dot(values, p.astype(BF16), preferred_element_type=F32)
            return (more, t) if o is None else (added + more, o + t)

        def step(h, n, high, after):
            m = jnp.max(high, axis=0, keepdims=True)
            high, added, o = None, None, None
            for j in parts:
                high = score(after, 1 - n, j, high)
                added, o = blend(h, n, j, m, added, o)
            added = jnp.sum(added, axis=0, keepdims=True)
            rows, row = head_rows(h), pl.ds(h, 1)
            halves = (slice(0, ROWS), slice(ROWS, 2 * ROWS))
            if not last:
                held[e, n, rows, :] = o
                tops[e, n, row, :] = m
                sums[e, n, row, :] = added
                return high
            m_old = tops[e, n, row, :]
            m_new = jnp.maximum(m, m_old)
            grow, keep = jnp.exp(m - m_new), jnp.exp(m_old - m_new)
            added = grow * added + keep * sums[e, n, row, :]
            inverse = 1.0 / added
            o = ((grow * inverse) * o + (keep * inverse) * held[e, n, rows, :]).astype(BF16)
            lse = m_new + jnp.log(added)
            for a in (0, 1):
                part[e, 2 * n + a, rows, :] = o[:, halves[a]]
                stat[e, 2 * n + a, row, :] = lse[:, halves[a]]
            return high

        def both_tiles(h, high):
            high = step(h, 0, high, h)
            return step(h, 1, high, jnp.minimum(h + 1, LOCAL_HEADS - 1))

        high = None
        for j in parts:
            high = score(0, 0, j, high)
        lax.fori_loop(0, LOCAL_HEADS, both_tiles, high)
        if last and e > 0:
            for j in range(4):
                send(("o", 4 - e, j), part.at[e, j], ret.at[(4 - e) - 1, j], at_z(e))
                send(("l", 4 - e, j), stat.at[e, j], rstat.at[(4 - e) - 1, j], at_z(e))

    for e in (0, 1, 3, 2):
        if e > 0:
            for j in range(4):
                arrive(("qz", e, j))
        attend(e, (0, 1, 3), False)
    arrive(("k", 2))
    turn_keys(2)
    arrive(("v", 2))
    attend(3, (2,), True)
    for j in range(4):
        if j > 0:
            arrive(("s", j))
        for h in range(LOCAL_HEADS):
            skt[j, h] = sx[j, 0, pl.ds(h * HEAD, HEAD), :].T
    for d in range(3):
        for j in range(4):
            slot = (j + 4 - (z + d) // 4) % 4
            half = pl.ds((j % 2) * ROWS, ROWS)
            for h in range(LOCAL_HEADS):
                kloc[d, j // 2, h, half, :] = skt[slot, h]
            vloc[d, j // 2, :, half] = sx[slot, 1]
    for e in (2, 1, 0):
        attend(e, (2, 4), True)

    for j in (2, 1, 3, 0):
        for b in (1, 2, 3):
            arrive(("o", b, j))
            arrive(("l", b, j))
        lses = [stat[0, j]] + [rstat[b, j] for b in range(3)]
        top = functools.reduce(jnp.maximum, lses)
        weights = [jnp.exp(v - top) for v in lses]
        inverse = 1.0 / sum(weights[1:], weights[0])
        coefs = [w * inverse for w in weights]
        for h in range(LOCAL_HEADS):
            rows = pl.ds(h * HEAD, HEAD)
            acc = coefs[0][h : h + 1, :] * part[0, j, rows, :].astype(F32)
            for b in range(3):
                acc += coefs[b + 1][h : h + 1, :] * ret[b, j, rows, :].astype(F32)
            merged[j, rows, :] = acc.astype(BF16)
        if j > 0:
            send(("a", 4 - j), merged.at[j], att.at[4 - j], at_x(j))
    mix_t[own, :] = merged[0]
    for j in (2, 1, 3):
        arrive(("a", j))
        mix_t[pl.ds(pl.multiple_of(((x + j) % 4) * HROWS, HROWS), HROWS), :] = att[j]

    loads["out"].wait()
    mix = jnp.concatenate([mix_t[pl.ds(b * 128, 128), :].T for b in range(10)], axis=1)
    attended = unit(jnp.dot(mix, wout[...], preferred_element_type=F32))
    hidden = hid[...]
    hidden = unit(hidden + arate_ref[...].reshape(1, D) * (attended - hidden))
    hid[...] = hidden
    upper, lower = pl.ds(0, ROWS), pl.ds(ROWS, ROWS)
    blocks[0, upper, :] = hidden.astype(BF16)

    halves = (pl.ds(0, 64), pl.ds(64, 64))
    mirror = (pl.ds(ROWS, 64), pl.ds(ROWS + 64, 64))
    send(("b", 3), blocks.at[0, upper], blocks.at[3, upper], at_y(1))
    send(("b", 1), blocks.at[0, upper], blocks.at[1, upper], at_y(3))
    send(("p", 0), blocks.at[0, upper], blocks.at[0, lower], partner)

    def swiglu(i):
        a = blocks[i]
        up = jnp.dot(a, wup[...], preferred_element_type=F32) * uscale_ref[...].reshape(1, -1)
        gate = jnp.dot(a, wgate[...], preferred_element_type=F32) * (gscale_ref[...].reshape(1, -1) * math.sqrt(D))
        act = (up * (gate / (1.0 + jnp.exp(-gate)))).astype(BF16)
        both = jnp.dot(act, wdown[...], preferred_element_type=F32)
        give[i] = both[ROWS:].astype(BF16)
        total[i] = both[:ROWS]
        send(("x", i), give.at[i], take.at[i], partner)

    def join(i):
        arrive(("x", i))
        both = total[i] + take[i].astype(F32)
        if i == 0:
            total[0] = both
        else:
            send_y[i - 1] = both.astype(BF16)
            send(("y", 4 - i), send_y.at[i - 1], recv_y.at[3 - i], at_y(i))

    for n in ("up", "gate", "down"):
        loads[n].wait()
    arrive(("p", 0))
    swiglu(0)
    arrive(("b", 3))
    send(("f", 0), blocks.at[3, halves[0]], blocks.at[2, halves[0]], at_y(1))
    send(("p", 3), blocks.at[3, upper], blocks.at[3, lower], partner)
    arrive(("b", 1))
    send(("f", 1), blocks.at[1, halves[1]], blocks.at[2, halves[1]], at_y(3))
    send(("p", 1), blocks.at[1, upper], blocks.at[1, lower], partner)
    arrive(("p", 3))
    swiglu(3)
    for k in (0, 1):
        arrive(("f", k))
        send(("g", k), blocks.at[2, halves[k]], blocks.at[2, mirror[k]], partner)
    arrive(("p", 1))
    join(3)
    swiglu(1)
    for k in (0, 1):
        arrive(("g", k))
    join(1)
    swiglu(2)
    join(2)
    join(0)
    summed = total[0]
    for i in (1, 3, 2):
        arrive(("y", i))
        summed += recv_y[i - 1].astype(F32)
    hidden = hid[...]
    hidden = unit(hidden + mrate_ref[...].reshape(1, D) * (unit(summed) - hidden))
    out_ref[...] = (math.sqrt(D) * hidden).astype(BF16)
    for copy in sends:
        copy.wait_send()


def body(
    tokens, seg_lengths, prefix_keys, prefix_values, w_qkv, w_out, qk_scale, attn_rate,
    w_up, w_gate, w_down, up_scale, gate_scale, mlp_rate,
):
    vmem = pl.BlockSpec(memory_space=pltpu.VMEM)
    smem = pl.BlockSpec(memory_space=pltpu.SMEM)
    hbm = pl.BlockSpec(memory_space=pltpu.HBM)
    ff = w_up.shape[1]
    vm = pltpu.VMEM
    out = pl.pallas_call(
        layer_kernel,
        out_shape=jax.ShapeDtypeStruct((ROWS, D), BF16),
        in_specs=[smem, hbm, hbm, hbm, hbm, hbm, vmem, vmem, hbm, hbm, hbm, vmem, vmem, vmem],
        out_specs=vmem,
        scratch_shapes=[
            vm((ROWS, D), BF16), vm((PREF, D), BF16), vm((PREF, D), BF16),
            vm((D, 3 * D), BF16), vm((D, D), BF16), vm((D, ff), BF16), vm((D, ff), BF16), vm((ff, D), BF16),
            vm((D, 128), F32),
            vm((D, PREF), BF16), vm((D, PREF), BF16), vm((D, ROWS), BF16), vm((2, D, ROWS), BF16),
            vm((4, HROWS, PREF), BF16), vm((4, HROWS, PREF), BF16), vm((4, HROWS, ROWS), BF16),
            vm((4, 2, HROWS, ROWS), BF16), vm((3, 4, HROWS, ROWS), BF16),
            vm((LOCAL_HEADS, 4 * PREF, HEAD), BF16), vm((4, LOCAL_HEADS, ROWS, HEAD), BF16),
            vm((16, 8, ROWS), jnp.int32), vm((3, 2, PREF, PREF), F32), vm((2, 5 * PREF, 2 * ROWS), F32),
            vm((3, 2, LOCAL_HEADS, PREF, HEAD), BF16), vm((3, 2, HROWS, PREF), BF16),
            vm((4, 2, HROWS, PREF), F32), vm((4, 2, 8, PREF), F32), vm((4, 2, 8, PREF), F32),
            vm((4, 4, HROWS, ROWS), BF16), vm((4, 4, 8, ROWS), F32),
            vm((3, 4, HROWS, ROWS), BF16), vm((3, 4, 8, ROWS), F32),
            vm((4, HROWS, ROWS), BF16), vm((4, HROWS, ROWS), BF16), vm((D, ROWS), BF16),
            vm((ROWS, D), F32), vm((4, 2 * ROWS, D), BF16), vm((4, ROWS, D), BF16), vm((4, ROWS, D), BF16),
            vm((4, ROWS, D), F32), vm((3, ROWS, D), BF16), vm((3, ROWS, D), BF16),
            pltpu.SemaphoreType.DMA((10,)), pltpu.SemaphoreType.DMA((140,)),
        ],
        compiler_params=pltpu.CompilerParams(
            collective_id=0, has_side_effects=True, vmem_limit_bytes=56 * 1024 * 1024
        ),
        name="layer",
    )(
        seg_lengths, tokens[0], prefix_keys[0], prefix_values[0], w_qkv, w_out, qk_scale, attn_rate,
        w_up, w_gate, w_down, up_scale, gate_scale, mlp_rate,
    )
    return out[None]


def solution(mesh):
    in_specs = (
        P("grp", "tok", None), P("grp", None), P("grp", "tok", None), P("grp", "tok", None),
        P(), P(), P(), P(), P(None, "grp"), P(None, "grp"), P("grp", None), P("grp"), P("grp"), P(),
    )
    return jax.shard_map(body, mesh=mesh, in_specs=in_specs, out_specs=P("grp", "tok", None), check_vma=False)
```

```python
import functools
import math

import jax
import jax.numpy as jnp
from jax import lax
from jax.experimental import pallas as pl
from jax.experimental.pallas import tpu as pltpu
from jax.sharding import PartitionSpec as P

D = 1280
HEAD = 64
LOCAL_HEADS = 5
HROWS = 320
ROWS = 128
PREF = 256
REQS = 32
EPS = 1e-06
MESH = pl.DeviceIdType.MESH
F32 = jnp.float32
BF16 = jnp.bfloat16


def unit(vector):
    return vector * lax.rsqrt(jnp.sum(vector * vector, axis=-1, keepdims=True) + EPS)


def head_unit(cols, scale):
    per_head = cols.reshape(2, HEAD, cols.shape[1])
    norm = lax.rsqrt(jnp.sum(per_head * per_head, axis=1, keepdims=True) + EPS)
    return (per_head * norm).reshape(cols.shape) * scale


def layer_kernel(
    lengths_ref, tok_hbm, pk_hbm, pv_hbm, wqkv_hbm, wout_hbm, scale_ref, arate_ref, wup_hbm, wgate_hbm, wdown_hbm,
    uscale_ref, gscale_ref, mrate_ref, out_ref,
    tok_ref, pk_ref, pv_ref, wqkv, wout, wup, wgate, wdown, scale_t,
    key_s, val_s, q_s, sk_s, kx, vx, qx, sx, qz, kt, skt, starts, mask, sbuf, kloc, vloc, held, tops, sums, part, stat, ret, rstat, merged, att, mix_t,
    hid, blocks, give, take, total, send_y, recv_y, w_sem, sem,
):
    tok, grp = lax.axis_index("tok"), lax.axis_index("grp")
    x, z = tok // 4, tok % 4
    y, c = grp // 2, grp % 2

    def at_x(i):
        return {"tok": ((x + i) % 4) * 4 + z}

    def at_z(i):
        return {"tok": x * 4 + (z + i) % 4}

    def at_y(i):
        return {"grp": ((y + i) % 4) * 2 + c}

    partner = {"grp": y * 2 + (1 - c)}
    used = [0]
    arrivals = {}
    sends = []

    def send(name, src, dst, dev):
        n = used[0]
        used[0] += 2
        copy = pltpu.make_async_remote_copy(
            src_ref=src, dst_ref=dst, send_sem=sem.at[n], recv_sem=sem.at[n + 1], device_id=dev, device_id_type=MESH
        )
        copy.start()
        sends.append(copy)
        assert name not in arrivals
        arrivals[name] = (dst, n)

    def arrive(name):
        dst, n = arrivals[name]
        pltpu.make_async_remote_copy(
            src_ref=dst, dst_ref=dst, send_sem=sem.at[n], recv_sem=sem.at[n + 1], device_id=partner,
            device_id_type=MESH,
        ).wait_recv()

    loads = {}

    def load(name, src, dst):
        copy = pltpu.make_async_copy(src, dst, w_sem.at[len(loads)])
        copy.start()
        loads[name] = copy

    load("pk", pk_hbm, pk_ref)
    load("tok", tok_hbm, tok_ref)
    load("pv", pv_hbm, pv_ref)
    barrier = pltpu.get_barrier_semaphore()
    for i in (1, 2, 3):
        for dev in (at_x(i), at_z(i), at_y(i)):
            pl.semaphore_signal(barrier, inc=1, device_id=dev, device_id_type=MESH)
    pl.semaphore_signal(barrier, inc=1, device_id=partner, device_id_type=MESH)
    for n in range(3):
        cols = pl.ds(n * D, D)
        load(n, wqkv_hbm.at[:, cols], wqkv.at[:, cols])
    load("out", wout_hbm, wout)
    load("up", wup_hbm, wup)
    load("gate", wgate_hbm, wgate)
    load("down", wdown_hbm, wdown)

    for b in range(10):
        lanes = pl.ds(b * 128, 128)
        scale_t[lanes, :] = jnp.broadcast_to(scale_ref[lanes].reshape(1, 128), (128, 128)).T
    loads["pk"].wait()
    for b in range(10):
        lanes = pl.ds(b * 128, 128)
        scale = scale_t[lanes, :]
        cols = pk_ref[:, lanes].astype(F32).T
        key_s[lanes, :] = head_unit(cols, jnp.concatenate([scale, scale], axis=1)).astype(BF16)
    pl.semaphore_wait(barrier, 10)

    def rows_of(ref, i):
        return ref.at[pl.ds(((x + i) % 4) * HROWS, HROWS), :]

    for i in (1, 3):
        send(("k", 4 - i), rows_of(key_s, i), kx.at[4 - i], at_x(i))

    loads["pv"].wait()
    for b in range(10):
        lanes = pl.ds(b * 128, 128)
        val_s[lanes, :] = pv_ref[:, lanes].T

    loads["tok"].wait()
    hidden = unit(tok_ref[...].astype(F32))
    hid[...] = hidden
    hidden = hidden.astype(BF16)

    def project(n, b):
        cols = jnp.dot(hidden, wqkv[:, n * D + b * 256 : n * D + b * 256 + 256], preferred_element_type=F32)
        return [cols[:, a * 128 : a * 128 + 128].T for a in (0, 1)]

    loads[0].wait()
    for b in range(5):
        for a, cols in enumerate(project(0, b)):
            lanes = pl.ds(b * 256 + a * 128, 128)
            query = head_unit(cols, scale_t[lanes, :]).astype(BF16)
            q_s[lanes, :] = query * BF16(math.sqrt(HEAD))
    for i in (2, 1, 3):
        send(("q", 4 - i), rows_of(q_s, i), qx.at[4 - i], at_x(i))
    qx[0] = q_s[pl.ds(pl.multiple_of(x * HROWS, HROWS), HROWS), :]

    def forward_q(j):
        for e in (1, 3):
            send(("qz", 4 - e, j), qx.at[j], qz.at[(4 - e) - 1, j], at_z(e))

    forward_q(0)
    for i in (1, 3):
        send(("v", 4 - i), rows_of(val_s, i), vx.at[4 - i], at_x(i))
    for n in (1, 2):
        loads[n].wait()
        for b in range(5):
            for a, cols in enumerate(project(n, b)):
                lanes = pl.ds(b * 256 + a * 128, 128)
                if n == 1:
                    cols = head_unit(cols, scale_t[lanes, :])
                sk_s[n - 1, lanes, :] = cols.astype(BF16)
    own = pl.ds(pl.multiple_of(x * HROWS, HROWS), HROWS)
    kx[0] = key_s[own, :]
    vx[0] = val_s[own, :]
    sx[0] = sk_s[:, own, :]

    position = (
        lax.broadcasted_iota(jnp.int32, (16, ROWS), 0) * ROWS + lax.broadcasted_iota(jnp.int32, (16, ROWS), 1)
    )
    end = jnp.int32(0)
    first = jnp.zeros((16, ROWS), jnp.int32)
    for r in range(REQS):
        end = end + lengths_ref[0, r]
        first = jnp.where(position >= end, end, first)
    for t in range(16):
        starts[t] = jnp.broadcast_to(first[t : t + 1, :], (8, ROWS))
    for e in range(3):
        for j in range(4):
            tq = ((x + j) % 4) * 4 + (z + e) % 4
            kpos = (tq - e) * ROWS + lax.broadcasted_iota(jnp.int32, (ROWS, ROWS), 0)
            qpos = tq * ROWS + lax.broadcasted_iota(jnp.int32, (ROWS, ROWS), 1)
            allowed = (kpos >= starts[tq, pl.ds(0, 1), :]) & (kpos <= qpos)
            bias = jnp.where(allowed, 0.0, -1e30)
            apart = jnp.full((ROWS, ROWS), -1e30, F32)
            mask[e, j // 2, pl.ds((j % 2) * ROWS, ROWS), :] = jnp.concatenate(
                [apart, bias] if j % 2 else [bias, apart], axis=1
            )
    for d in range(4):
        for j in range(4):
            stat[d, j] = jnp.zeros((8, ROWS), F32)

    def turn_keys(j):
        for h in range(LOCAL_HEADS):
            kt[h, pl.ds(j * PREF, PREF), :] = kx[j, pl.ds(h * HEAD, HEAD), :].T

    turn_keys(0)
    for j in (1, 3):
        arrive(("k", j))
        turn_keys(j)
    for j in (1, 3, 2):
        arrive(("q", j))
        forward_q(j)
    for j in (1, 3):
        arrive(("v", j))
    send(("k", 2), rows_of(key_s, 2), kx.at[2], at_x(2))
    send(("v", 2), rows_of(val_s, 2), vx.at[2], at_x(2))

    def fold(v):
        return v.reshape(v.shape[0] // 8, 8, v.shape[1])

    def attend(e, parts, last):
        def head_rows(h):
            return pl.ds(pl.multiple_of(h * HEAD, HEAD), HEAD)

        def score(h, n, j, high):
            j0, rows = 2 * n, head_rows(h)
            q = [qx[j0 + a, rows, :] if e == 0 else qz[e - 1, j0 + a, rows, :] for a in (0, 1)]
            keys = kt[h, pl.ds(j * PREF, PREF), :] if j < 4 else kloc[e, n, h]
            s = jnp.dot(keys, jnp.concatenate(q, axis=1), preferred_element_type=F32)
            if j == 4:
                s = s + mask[e, n]
            sbuf[n, pl.ds(j * PREF, PREF), :] = s
            top = jnp.max(fold(s), axis=0)
            return top if high is None else jnp.maximum(high, top)

        def blend(h, n, j, m, added, o):
            rows = head_rows(h)
            p = jnp.exp(sbuf[n, pl.ds(j * PREF, PREF), :] - m)
            more = jnp.sum(fold(p), axis=0)
            values = vx[j, rows, :] if j < 4 else vloc[e, n, rows, :]
            t = jnp.dot(values, p.astype(BF16), preferred_element_type=F32)
            return (more, t) if o is None else (added + more, o + t)

        def step(h, n, high, after):
            m = jnp.max(high, axis=0, keepdims=True)
            high, added, o = None, None, None
            for j in parts:
                high = score(after, 1 - n, j, high)
                added, o = blend(h, n, j, m, added, o)
            added = jnp.sum(added, axis=0, keepdims=True)
            rows, row = head_rows(h), pl.ds(h, 1)
            halves = (slice(0, ROWS), slice(ROWS, 2 * ROWS))
            if not last:
                held[e, n, rows, :] = o
                tops[e, n, row, :] = m
                sums[e, n, row, :] = added
                return high
            if e < 3:
                m_old = tops[e, n, row, :]
                m_new = jnp.maximum(m, m_old)
                grow, keep = jnp.exp(m - m_new), jnp.exp(m_old - m_new)
                added = grow * added + keep * sums[e, n, row, :]
                inverse = 1.0 / added
                o = ((grow * inverse) * o + (keep * inverse) * held[e, n, rows, :]).astype(BF16)
                m = m_new
            else:
                o = (o * (1.0 / added)).astype(BF16)
            lse = m + jnp.log(added)
            for a in (0, 1):
                part[e, 2 * n + a, rows, :] = o[:, halves[a]]
                stat[e, 2 * n + a, row, :] = lse[:, halves[a]]
            return high

        def both_tiles(h, high):
            high = step(h, 0, high, h)
            return step(h, 1, high, jnp.minimum(h + 1, LOCAL_HEADS - 1))

        high = None
        for j in parts:
            high = score(0, 0, j, high)
        lax.fori_loop(0, LOCAL_HEADS, both_tiles, high)
        if last and e > 0:
            for j in (2, 1, 3, 0):
                send(("o", 4 - e, j), part.at[e, j], ret.at[(4 - e) - 1, j], at_z(e))
                send(("l", 4 - e, j), stat.at[e, j], rstat.at[(4 - e) - 1, j], at_z(e))

    def queries_here(e):
        for j in range(4):
            arrive(("qz", e, j))

    attend(0, (0, 1, 3), False)
    for j in (0, 1, 3, 2):
        send(("qz", 2, j), qx.at[j], qz.at[1, j], at_z(2))
    queries_here(1)
    attend(1, (0, 1, 3), False)
    for i in (2, 1, 3):
        src = sk_s.at[:, pl.ds(((x + i) % 4) * HROWS, HROWS), :]
        send(("s", 4 - i), src, sx.at[4 - i], at_x(i))
    arrive(("k", 2))
    turn_keys(2)
    arrive(("v", 2))
    queries_here(3)
    attend(3, (0, 1, 3, 2), True)
    queries_here(2)
    attend(2, (0, 1, 3), False)
    for j in range(4):
        if j > 0:
            arrive(("s", j))
        for h in range(LOCAL_HEADS):
            skt[j, h] = sx[j, 0, pl.ds(h * HEAD, HEAD), :].T
    for d in range(3):
        for j in range(4):
            slot = (j + 4 - (z + d) // 4) % 4
            half = pl.ds((j % 2) * ROWS, ROWS)
            for h in range(LOCAL_HEADS):
                kloc[d, j // 2, h, half, :] = skt[slot, h]
            vloc[d, j // 2, :, half] = sx[slot, 1]
    for e in (1, 2, 0):
        attend(e, (2, 4), True)

    for j in (2, 1, 3, 0):
        for b in (1, 2, 3):
            arrive(("o", b, j))
            arrive(("l", b, j))
        lses = [stat[0, j]] + [rstat[b, j] for b in range(3)]
        top = functools.reduce(jnp.maximum, lses)
        weights = [jnp.exp(v - top) for v in lses]
        inverse = 1.0 / sum(weights[1:], weights[0])
        coefs = [w * inverse for w in weights]
        for h in range(LOCAL_HEADS):
            rows = pl.ds(h * HEAD, HEAD)
            acc = coefs[0][h : h + 1, :] * part[0, j, rows, :].astype(F32)
            for b in range(3):
                acc += coefs[b + 1][h : h + 1, :] * ret[b, j, rows, :].astype(F32)
            merged[j, rows, :] = acc.astype(BF16)
        if j > 0:
            send(("a", 4 - j), merged.at[j], att.at[4 - j], at_x(j))
    mix_t[own, :] = merged[0]
    for j in (2, 1, 3):
        arrive(("a", j))
        mix_t[pl.ds(pl.multiple_of(((x + j) % 4) * HROWS, HROWS), HROWS), :] = att[j]

    loads["out"].wait()
    mix = jnp.concatenate([mix_t[pl.ds(b * 128, 128), :].T for b in range(10)], axis=1)
    attended = unit(jnp.dot(mix, wout[...], preferred_element_type=F32))
    hidden = hid[...]
    hidden = unit(hidden + arate_ref[...].reshape(1, D) * (attended - hidden))
    hid[...] = hidden
    upper, lower = pl.ds(0, ROWS), pl.ds(ROWS, ROWS)
    blocks[0, upper, :] = hidden.astype(BF16)

    halves = (pl.ds(0, 64), pl.ds(64, 64))
    ours, theirs = (pl.ds(0, 64), pl.ds(ROWS, 64)), (pl.ds(64, 64), pl.ds(ROWS + 64, 64))
    for i, k in ((3, 0), (1, 1), (3, 1), (1, 0)):
        send(("b", i, k), blocks.at[0, halves[k]], blocks.at[i, ours[k]], at_y(4 - i))
    send(("p", 0), blocks.at[0, upper], blocks.at[0, lower], partner)

    def share(i, k):
        send(("p", i, k), blocks.at[i, ours[k]], blocks.at[i, theirs[k]], partner)

    def swiglu(i, rows):
        size = rows.size // 2
        mine = pl.ds(rows.start // 2, size)
        a = blocks[i, rows, :]
        up = jnp.dot(a, wup[...], preferred_element_type=F32) * uscale_ref[...].reshape(1, -1)
        gate = jnp.dot(a, wgate[...], preferred_element_type=F32) * (gscale_ref[...].reshape(1, -1) * math.sqrt(D))
        act = (up * (gate / (1.0 + jnp.exp(-gate)))).astype(BF16)
        both = jnp.dot(act, wdown[...], preferred_element_type=F32)
        give[i, mine, :] = both[size:].astype(BF16)
        total[i, mine, :] = both[:size]
        send(("x", i, rows.start), give.at[i, mine], take.at[i, mine], partner)

    def join(i, rows):
        mine = pl.ds(rows.start // 2, rows.size // 2)
        arrive(("x", i, rows.start))
        both = total[i, mine, :] + take[i, mine, :].astype(F32)
        if i == 0:
            total[0] = both
        else:
            send_y[i - 1, mine, :] = both.astype(BF16)
            send(("y", 4 - i, rows.start), send_y.at[i - 1, mine], recv_y.at[3 - i, mine], at_y(i))

    whole, parts = pl.ds(0, 2 * ROWS), (pl.ds(0, ROWS), pl.ds(ROWS, ROWS))
    for n in ("up", "gate", "down"):
        loads[n].wait()
    arrive(("p", 0))
    swiglu(0, whole)
    for i, k in ((3, 0), (1, 1)):
        arrive(("b", i, k))
        send(("b", 2, k), blocks.at[i, ours[k]], blocks.at[2, ours[k]], at_y(4 - i))
        share(i, k)
    held_back = None
    for i, k in ((3, 0), (1, 1), (3, 1), (1, 0), (2, 0), (2, 1)):
        if (i, k) == (1, 1):
            for pair in ((3, 1), (1, 0)):
                arrive(("b",) + pair)
                share(*pair)
        if (i, k) == (1, 0):
            for pair in ((2, 0), (2, 1)):
                arrive(("b",) + pair)
                share(*pair)
        arrive(("p", i, k))
        swiglu(i, parts[k])
        if held_back is not None:
            join(*held_back)
        held_back = (i, parts[k])
    join(*held_back)
    join(0, whole)
    summed = total[0]
    for i in (1, 3, 2):
        arrive(("y", i, 0))
        arrive(("y", i, ROWS))
        summed += recv_y[i - 1].astype(F32)
    hidden = hid[...]
    hidden = unit(hidden + mrate_ref[...].reshape(1, D) * (unit(summed) - hidden))
    out_ref[...] = (math.sqrt(D) * hidden).astype(BF16)
    for copy in sends:
        copy.wait_send()


def body(
    tokens, seg_lengths, prefix_keys, prefix_values, w_qkv, w_out, qk_scale, attn_rate,
    w_up, w_gate, w_down, up_scale, gate_scale, mlp_rate,
):
    vmem = pl.BlockSpec(memory_space=pltpu.VMEM)
    smem = pl.BlockSpec(memory_space=pltpu.SMEM)
    hbm = pl.BlockSpec(memory_space=pltpu.HBM)
    ff = w_up.shape[1]
    vm = pltpu.VMEM
    out = pl.pallas_call(
        layer_kernel,
        out_shape=jax.ShapeDtypeStruct((ROWS, D), BF16),
        in_specs=[smem, hbm, hbm, hbm, hbm, hbm, vmem, vmem, hbm, hbm, hbm, vmem, vmem, vmem],
        out_specs=vmem,
        scratch_shapes=[
            vm((ROWS, D), BF16), vm((PREF, D), BF16), vm((PREF, D), BF16),
            vm((D, 3 * D), BF16), vm((D, D), BF16), vm((D, ff), BF16), vm((D, ff), BF16), vm((ff, D), BF16),
            vm((D, 128), F32),
            vm((D, PREF), BF16), vm((D, PREF), BF16), vm((D, ROWS), BF16), vm((2, D, ROWS), BF16),
            vm((4, HROWS, PREF), BF16), vm((4, HROWS, PREF), BF16), vm((4, HROWS, ROWS), BF16),
            vm((4, 2, HROWS, ROWS), BF16), vm((3, 4, HROWS, ROWS), BF16),
            vm((LOCAL_HEADS, 4 * PREF, HEAD), BF16), vm((4, LOCAL_HEADS, ROWS, HEAD), BF16),
            vm((16, 8, ROWS), jnp.int32), vm((3, 2, PREF, PREF), F32), vm((2, 5 * PREF, 2 * ROWS), F32),
            vm((3, 2, LOCAL_HEADS, PREF, HEAD), BF16), vm((3, 2, HROWS, PREF), BF16),
            vm((3, 2, HROWS, PREF), F32), vm((3, 2, 8, PREF), F32), vm((3, 2, 8, PREF), F32),
            vm((4, 4, HROWS, ROWS), BF16), vm((4, 4, 8, ROWS), F32),
            vm((3, 4, HROWS, ROWS), BF16), vm((3, 4, 8, ROWS), F32),
            vm((4, HROWS, ROWS), BF16), vm((4, HROWS, ROWS), BF16), vm((D, ROWS), BF16),
            vm((ROWS, D), F32), vm((4, 2 * ROWS, D), BF16), vm((4, ROWS, D), BF16), vm((4, ROWS, D), BF16),
            vm((4, ROWS, D), F32), vm((3, ROWS, D), BF16), vm((3, ROWS, D), BF16),
            pltpu.SemaphoreType.DMA((10,)), pltpu.SemaphoreType.DMA((168,)),
        ],
        compiler_params=pltpu.CompilerParams(
            collective_id=0, has_side_effects=True, vmem_limit_bytes=56 * 1024 * 1024
        ),
        name="layer",
    )(
        seg_lengths, tokens[0], prefix_keys[0], prefix_values[0], w_qkv, w_out, qk_scale, attn_rate,
        w_up, w_gate, w_down, up_scale, gate_scale, mlp_rate,
    )
    return out[None]


def solution(mesh):
    in_specs = (
        P("grp", "tok", None), P("grp", None), P("grp", "tok", None), P("grp", "tok", None),
        P(), P(), P(), P(), P(None, "grp"), P(None, "grp"), P("grp", None), P("grp"), P("grp"), P(),
    )
    return jax.shard_map(body, mesh=mesh, in_specs=in_specs, out_specs=P("grp", "tok", None), check_vma=False)
```

```python
import functools
import math

import jax
import jax.numpy as jnp
from jax import lax
from jax.experimental import pallas as pl
from jax.experimental.pallas import tpu as pltpu
from jax.sharding import PartitionSpec as P

D = 1280
HEAD = 64
LOCAL_HEADS = 5
HROWS = 320
ROWS = 128
PREF = 256
REQS = 32
EPS = 1e-06
MESH = pl.DeviceIdType.MESH
F32 = jnp.float32
BF16 = jnp.bfloat16


def unit(vector):
    return vector * lax.rsqrt(jnp.sum(vector * vector, axis=-1, keepdims=True) + EPS)


def head_unit(cols, scale):
    per_head = cols.reshape(2, HEAD, cols.shape[1])
    norm = lax.rsqrt(jnp.sum(per_head * per_head, axis=1, keepdims=True) + EPS)
    return (per_head * norm).reshape(cols.shape) * scale


def layer_kernel(
    lengths_ref, tok_hbm, pk_hbm, pv_hbm, wqkv_hbm, wout_hbm, scale_ref, arate_ref, wup_hbm, wgate_hbm, wdown_hbm,
    uscale_ref, gscale_ref, mrate_ref, out_ref,
    tok_ref, pk_ref, pv_ref, wqkv, wout, wup, wgate, wdown, scale_t,
    key_s, val_s, q_s, sk_s, kx, vx, qx, sx, qz, kt, skt, starts, mask, sbuf, kloc, vloc, held, tops, sums, part, stat, ret, rstat, merged, att, mix_t,
    hid, blocks, give, take, total, send_y, recv_y, passing, w_sem, sem,
):
    tok, grp = lax.axis_index("tok"), lax.axis_index("grp")
    x, z = tok // 4, tok % 4
    y, c = grp // 2, grp % 2

    def at_x(i):
        return {"tok": ((x + i) % 4) * 4 + z}

    def at_z(i):
        return {"tok": x * 4 + (z + i) % 4}

    def at_y(i):
        return {"grp": ((y + i) % 4) * 2 + c}

    partner = {"grp": y * 2 + (1 - c)}
    used = [0]
    arrivals = {}
    sends = []

    def send(name, src, dst, dev):
        n = used[0]
        used[0] += 2
        copy = pltpu.make_async_remote_copy(
            src_ref=src, dst_ref=dst, send_sem=sem.at[n], recv_sem=sem.at[n + 1], device_id=dev, device_id_type=MESH
        )
        copy.start()
        sends.append(copy)
        assert name not in arrivals
        arrivals[name] = (dst, n)

    def arrive(name):
        dst, n = arrivals[name]
        pltpu.make_async_remote_copy(
            src_ref=dst, dst_ref=dst, send_sem=sem.at[n], recv_sem=sem.at[n + 1], device_id=partner,
            device_id_type=MESH,
        ).wait_recv()

    loads = {}

    def load(name, src, dst):
        copy = pltpu.make_async_copy(src, dst, w_sem.at[len(loads)])
        copy.start()
        loads[name] = copy

    load("pk", pk_hbm, pk_ref)
    load("tok", tok_hbm, tok_ref)
    load("pv", pv_hbm, pv_ref)
    barrier = pltpu.get_barrier_semaphore()
    for i in (1, 2, 3):
        for dev in (at_x(i), at_z(i), at_y(i)):
            pl.semaphore_signal(barrier, inc=1, device_id=dev, device_id_type=MESH)
    pl.semaphore_signal(barrier, inc=1, device_id=partner, device_id_type=MESH)
    for n in range(3):
        cols = pl.ds(n * D, D)
        load(n, wqkv_hbm.at[:, cols], wqkv.at[:, cols])
    load("out", wout_hbm, wout)
    load("up", wup_hbm, wup)
    load("gate", wgate_hbm, wgate)
    load("down", wdown_hbm, wdown)

    for b in range(10):
        lanes = pl.ds(b * 128, 128)
        scale_t[lanes, :] = jnp.broadcast_to(scale_ref[lanes].reshape(1, 128), (128, 128)).T
    loads["pk"].wait()
    for b in range(10):
        lanes = pl.ds(b * 128, 128)
        scale = scale_t[lanes, :]
        cols = pk_ref[:, lanes].astype(F32).T
        key_s[lanes, :] = head_unit(cols, jnp.concatenate([scale, scale], axis=1)).astype(BF16)
    pl.semaphore_wait(barrier, 10)

    def rows_of(ref, i):
        return ref.at[pl.ds(((x + i) % 4) * HROWS, HROWS), :]

    for i in (1, 3):
        send(("k", 4 - i), rows_of(key_s, i), kx.at[4 - i], at_x(i))

    loads["pv"].wait()
    for b in range(10):
        lanes = pl.ds(b * 128, 128)
        val_s[lanes, :] = pv_ref[:, lanes].T

    loads["tok"].wait()
    hidden = unit(tok_ref[...].astype(F32))
    hid[...] = hidden
    hidden = hidden.astype(BF16)

    def project(n, b):
        cols = jnp.dot(hidden, wqkv[:, n * D + b * 256 : n * D + b * 256 + 256], preferred_element_type=F32)
        return [cols[:, a * 128 : a * 128 + 128].T for a in (0, 1)]

    loads[0].wait()
    for b in range(5):
        for a, cols in enumerate(project(0, b)):
            lanes = pl.ds(b * 256 + a * 128, 128)
            query = head_unit(cols, scale_t[lanes, :]).astype(BF16)
            q_s[lanes, :] = query * BF16(math.sqrt(HEAD))
    for i in (2, 1, 3):
        send(("q", 4 - i), rows_of(q_s, i), qx.at[4 - i], at_x(i))
    qx[0] = q_s[pl.ds(pl.multiple_of(x * HROWS, HROWS), HROWS), :]

    def forward_q(j):
        for e in (1, 3):
            send(("qz", 4 - e, j), qx.at[j], qz.at[(4 - e) - 1, j], at_z(e))

    forward_q(0)
    for i in (1, 3):
        send(("v", 4 - i), rows_of(val_s, i), vx.at[4 - i], at_x(i))
    for n in (1, 2):
        loads[n].wait()
        for b in range(5):
            for a, cols in enumerate(project(n, b)):
                lanes = pl.ds(b * 256 + a * 128, 128)
                if n == 1:
                    cols = head_unit(cols, scale_t[lanes, :])
                sk_s[n - 1, lanes, :] = cols.astype(BF16)
    own = pl.ds(pl.multiple_of(x * HROWS, HROWS), HROWS)
    kx[0] = key_s[own, :]
    vx[0] = val_s[own, :]
    sx[0] = sk_s[:, own, :]

    position = (
        lax.broadcasted_iota(jnp.int32, (16, ROWS), 0) * ROWS + lax.broadcasted_iota(jnp.int32, (16, ROWS), 1)
    )
    end = jnp.int32(0)
    first = jnp.zeros((16, ROWS), jnp.int32)
    for r in range(REQS):
        end = end + lengths_ref[0, r]
        first = jnp.where(position >= end, end, first)
    for t in range(16):
        starts[t] = jnp.broadcast_to(first[t : t + 1, :], (8, ROWS))
    for e in range(3):
        for j in range(4):
            tq = ((x + j) % 4) * 4 + (z + e) % 4
            kpos = (tq - e) * ROWS + lax.broadcasted_iota(jnp.int32, (ROWS, ROWS), 0)
            qpos = tq * ROWS + lax.broadcasted_iota(jnp.int32, (ROWS, ROWS), 1)
            allowed = (kpos >= starts[tq, pl.ds(0, 1), :]) & (kpos <= qpos)
            bias = jnp.where(allowed, 0.0, -1e30)
            apart = jnp.full((ROWS, ROWS), -1e30, F32)
            mask[e, j // 2, pl.ds((j % 2) * ROWS, ROWS), :] = jnp.concatenate(
                [apart, bias] if j % 2 else [bias, apart], axis=1
            )
    for d in range(4):
        for j in range(4):
            stat[d, j] = jnp.zeros((8, ROWS), F32)

    def turn_keys(j):
        for h in range(LOCAL_HEADS):
            kt[h, pl.ds(j * PREF, PREF), :] = kx[j, pl.ds(h * HEAD, HEAD), :].T

    turn_keys(0)
    for j in (1, 3):
        arrive(("k", j))
        turn_keys(j)
    for j in (1, 3, 2):
        arrive(("q", j))
        forward_q(j)
    send(("k", 2), rows_of(key_s, 2), kx.at[2], at_x(2))
    send(("v", 2), rows_of(val_s, 2), vx.at[2], at_x(2))

    for j in (1, 3):
        arrive(("v", j))

    def fold(v):
        return v.reshape(v.shape[0] // 8, 8, v.shape[1])

    def attend(e, parts, last):
        def head_rows(h):
            return pl.ds(pl.multiple_of(h * HEAD, HEAD), HEAD)

        def score(h, n, j, high):
            j0, rows = 2 * n, head_rows(h)
            q = [qx[j0 + a, rows, :] if e == 0 else qz[e - 1, j0 + a, rows, :] for a in (0, 1)]
            keys = kt[h, pl.ds(j * PREF, PREF), :] if j < 4 else kloc[e, n, h]
            s = jnp.dot(keys, jnp.concatenate(q, axis=1), preferred_element_type=F32)
            if j == 4:
                s = s + mask[e, n]
            sbuf[n, pl.ds(j * PREF, PREF), :] = s
            top = jnp.max(fold(s), axis=0)
            return top if high is None else jnp.maximum(high, top)

        def blend(h, n, j, m, added, o):
            rows = head_rows(h)
            p = jnp.exp(sbuf[n, pl.ds(j * PREF, PREF), :] - m)
            more = jnp.sum(fold(p), axis=0)
            values = vx[j, rows, :] if j < 4 else vloc[e, n, rows, :]
            t = jnp.dot(values, p.astype(BF16), preferred_element_type=F32)
            return (more, t) if o is None else (added + more, o + t)

        def step(h, n, high, after):
            m = jnp.max(high, axis=0, keepdims=True)
            high, added, o = None, None, None
            for j in parts:
                high = score(after, 1 - n, j, high)
                added, o = blend(h, n, j, m, added, o)
            added = jnp.sum(added, axis=0, keepdims=True)
            rows, row = head_rows(h), pl.ds(h, 1)
            halves = (slice(0, ROWS), slice(ROWS, 2 * ROWS))
            if not last:
                held[e, n, rows, :] = o
                tops[e, n, row, :] = m
                sums[e, n, row, :] = added
                return high
            if e < 3:
                m_old = tops[e, n, row, :]
                m_new = jnp.maximum(m, m_old)
                grow, keep = jnp.exp(m - m_new), jnp.exp(m_old - m_new)
                added = grow * added + keep * sums[e, n, row, :]
                inverse = 1.0 / added
                o = ((grow * inverse) * o + (keep * inverse) * held[e, n, rows, :]).astype(BF16)
                m = m_new
            else:
                o = (o * (1.0 / added)).astype(BF16)
            lse = m + jnp.log(added)
            for a in (0, 1):
                part[e, 2 * n + a, rows, :] = o[:, halves[a]]
                stat[e, 2 * n + a, row, :] = lse[:, halves[a]]
            return high

        def both_tiles(h, high):
            high = step(h, 0, high, h)
            return step(h, 1, high, jnp.minimum(h + 1, LOCAL_HEADS - 1))

        high = None
        for j in parts:
            high = score(0, 0, j, high)
        lax.fori_loop(0, LOCAL_HEADS, both_tiles, high)
        if last and e > 0:
            for j in (2, 1, 3, 0):
                send(("o", 4 - e, j), part.at[e, j], ret.at[(4 - e) - 1, j], at_z(e))
                send(("l", 4 - e, j), stat.at[e, j], rstat.at[(4 - e) - 1, j], at_z(e))

    def queries_here(e):
        for j in range(4):
            arrive(("qz", e, j))

    for j in (0, 1, 3, 2):
        send(("qz", 2, j), qx.at[j], qz.at[1, j], at_z(2))
    attend(0, (0, 1, 3), False)
    queries_here(1)
    attend(1, (0, 1, 3), False)
    for i in (2, 1, 3):
        src = sk_s.at[:, pl.ds(((x + i) % 4) * HROWS, HROWS), :]
        send(("s", 4 - i), src, sx.at[4 - i], at_x(i))
    arrive(("k", 2))
    turn_keys(2)
    arrive(("v", 2))
    queries_here(3)
    attend(3, (0, 1, 3, 2), True)
    queries_here(2)
    attend(2, (0, 1, 3), False)
    for j in range(4):
        if j > 0:
            arrive(("s", j))
        for h in range(LOCAL_HEADS):
            skt[j, h] = sx[j, 0, pl.ds(h * HEAD, HEAD), :].T
    for d in range(3):
        for j in range(4):
            slot = (j + 4 - (z + d) // 4) % 4
            half = pl.ds((j % 2) * ROWS, ROWS)
            for h in range(LOCAL_HEADS):
                kloc[d, j // 2, h, half, :] = skt[slot, h]
            vloc[d, j // 2, :, half] = sx[slot, 1]
    for e in (1, 2, 0):
        attend(e, (2, 4), True)

    for j in (2, 1, 3, 0):
        for b in (1, 2, 3):
            arrive(("o", b, j))
            arrive(("l", b, j))
        lses = [stat[0, j]] + [rstat[b, j] for b in range(3)]
        top = functools.reduce(jnp.maximum, lses)
        weights = [jnp.exp(v - top) for v in lses]
        inverse = 1.0 / sum(weights[1:], weights[0])
        coefs = [w * inverse for w in weights]
        for h in range(LOCAL_HEADS):
            rows = pl.ds(h * HEAD, HEAD)
            acc = coefs[0][h : h + 1, :] * part[0, j, rows, :].astype(F32)
            for b in range(3):
                acc += coefs[b + 1][h : h + 1, :] * ret[b, j, rows, :].astype(F32)
            merged[j, rows, :] = acc.astype(BF16)
        if j > 0:
            send(("a", 4 - j), merged.at[j], att.at[4 - j], at_x(j))
    mix_t[own, :] = merged[0]
    for j in (2, 1, 3):
        arrive(("a", j))
        mix_t[pl.ds(pl.multiple_of(((x + j) % 4) * HROWS, HROWS), HROWS), :] = att[j]

    loads["out"].wait()
    mix = jnp.concatenate([mix_t[pl.ds(b * 128, 128), :].T for b in range(10)], axis=1)
    attended = unit(jnp.dot(mix, wout[...], preferred_element_type=F32))
    hidden = hid[...]
    hidden = unit(hidden + arate_ref[...].reshape(1, D) * (attended - hidden))
    hid[...] = hidden
    upper, lower = pl.ds(0, ROWS), pl.ds(ROWS, ROWS)
    blocks[0, upper, :] = hidden.astype(BF16)

    halves = (pl.ds(0, 64), pl.ds(64, 64))
    ours, theirs = (pl.ds(0, 64), pl.ds(ROWS, 64)), (pl.ds(64, 64), pl.ds(ROWS + 64, 64))
    for i, k in ((3, 0), (1, 1), (3, 1), (1, 0)):
        send(("b", i, k), blocks.at[0, halves[k]], blocks.at[i, ours[k]], at_y(4 - i))
    send(("p", 0), blocks.at[0, upper], blocks.at[0, lower], partner)

    def share(i, k):
        send(("p", i, k), blocks.at[i, ours[k]], blocks.at[i, theirs[k]], partner)

    def swiglu(i, rows):
        size = rows.size // 2
        mine = pl.ds(rows.start // 2, size)
        a = blocks[i, rows, :]
        up = jnp.dot(a, wup[...], preferred_element_type=F32) * uscale_ref[...].reshape(1, -1)
        gate = jnp.dot(a, wgate[...], preferred_element_type=F32) * (gscale_ref[...].reshape(1, -1) * math.sqrt(D))
        act = (up * (gate / (1.0 + jnp.exp(-gate)))).astype(BF16)
        both = jnp.dot(act, wdown[...], preferred_element_type=F32)
        give[i, mine, :] = both[size:].astype(BF16)
        total[i, mine, :] = both[:size]
        send(("x", i, rows.start), give.at[i, mine], take.at[i, mine], partner)

    def join(i, rows):
        mine = pl.ds(rows.start // 2, rows.size // 2)
        arrive(("x", i, rows.start))
        both = total[i, mine, :] + take[i, mine, :].astype(F32)
        k = rows.start // ROWS
        if i == 0:
            total[0] = both
        elif i == 2:
            send_y[1, mine, :] = both.astype(BF16)
            send(("m", k), send_y.at[1, mine], passing.at[k], at_y((1, 3)[k]))
        else:
            if (i, k) in ((1, 0), (3, 1)):
                arrive(("m", k))
                both += passing[k].astype(F32)
            send_y[i - 1, mine, :] = both.astype(BF16)
            send(("y", 4 - i, rows.start), send_y.at[i - 1, mine], recv_y.at[3 - i, mine], at_y(i))

    whole, parts = pl.ds(0, 2 * ROWS), (pl.ds(0, ROWS), pl.ds(ROWS, ROWS))
    for n in ("up", "gate", "down"):
        loads[n].wait()
    arrive(("p", 0))
    swiglu(0, whole)
    for i, k in ((3, 0), (1, 1)):
        arrive(("b", i, k))
        send(("b", 2, k), blocks.at[i, ours[k]], blocks.at[2, ours[k]], at_y(4 - i))
        share(i, k)
    held_back = None
    for i, k in ((3, 0), (1, 1), (2, 0), (2, 1), (1, 0), (3, 1)):
        if (i, k) == (1, 1):
            for pair in ((3, 1), (1, 0)):
                arrive(("b",) + pair)
                share(*pair)
        if (i, k) == (2, 0):
            for pair in ((2, 0), (2, 1)):
                arrive(("b",) + pair)
                share(*pair)
        arrive(("p", i, k))
        swiglu(i, parts[k])
        if held_back is not None:
            join(*held_back)
        held_back = (i, parts[k])
    join(*held_back)
    join(0, whole)
    summed = total[0]
    for i in (1, 3):
        arrive(("y", i, 0))
        arrive(("y", i, ROWS))
        summed += recv_y[i - 1].astype(F32)
    hidden = hid[...]
    hidden = unit(hidden + mrate_ref[...].reshape(1, D) * (unit(summed) - hidden))
    out_ref[...] = (math.sqrt(D) * hidden).astype(BF16)
    for copy in sends:
        copy.wait_send()


def body(
    tokens, seg_lengths, prefix_keys, prefix_values, w_qkv, w_out, qk_scale, attn_rate,
    w_up, w_gate, w_down, up_scale, gate_scale, mlp_rate,
):
    vmem = pl.BlockSpec(memory_space=pltpu.VMEM)
    smem = pl.BlockSpec(memory_space=pltpu.SMEM)
    hbm = pl.BlockSpec(memory_space=pltpu.HBM)
    ff = w_up.shape[1]
    vm = pltpu.VMEM
    out = pl.pallas_call(
        layer_kernel,
        out_shape=jax.ShapeDtypeStruct((ROWS, D), BF16),
        in_specs=[smem, hbm, hbm, hbm, hbm, hbm, vmem, vmem, hbm, hbm, hbm, vmem, vmem, vmem],
        out_specs=vmem,
        scratch_shapes=[
            vm((ROWS, D), BF16), vm((PREF, D), BF16), vm((PREF, D), BF16),
            vm((D, 3 * D), BF16), vm((D, D), BF16), vm((D, ff), BF16), vm((D, ff), BF16), vm((ff, D), BF16),
            vm((D, 128), F32),
            vm((D, PREF), BF16), vm((D, PREF), BF16), vm((D, ROWS), BF16), vm((2, D, ROWS), BF16),
            vm((4, HROWS, PREF), BF16), vm((4, HROWS, PREF), BF16), vm((4, HROWS, ROWS), BF16),
            vm((4, 2, HROWS, ROWS), BF16), vm((3, 4, HROWS, ROWS), BF16),
            vm((LOCAL_HEADS, 4 * PREF, HEAD), BF16), vm((4, LOCAL_HEADS, ROWS, HEAD), BF16),
            vm((16, 8, ROWS), jnp.int32), vm((3, 2, PREF, PREF), F32), vm((2, 5 * PREF, 2 * ROWS), F32),
            vm((3, 2, LOCAL_HEADS, PREF, HEAD), BF16), vm((3, 2, HROWS, PREF), BF16),
            vm((3, 2, HROWS, PREF), F32), vm((3, 2, 8, PREF), F32), vm((3, 2, 8, PREF), F32),
            vm((4, 4, HROWS, ROWS), BF16), vm((4, 4, 8, ROWS), F32),
            vm((3, 4, HROWS, ROWS), BF16), vm((3, 4, 8, ROWS), F32),
            vm((4, HROWS, ROWS), BF16), vm((4, HROWS, ROWS), BF16), vm((D, ROWS), BF16),
            vm((ROWS, D), F32), vm((4, 2 * ROWS, D), BF16), vm((4, ROWS, D), BF16), vm((4, ROWS, D), BF16),
            vm((4, ROWS, D), F32), vm((3, ROWS, D), BF16), vm((3, ROWS, D), BF16),
            vm((2, ROWS // 2, D), BF16),
            pltpu.SemaphoreType.DMA((10,)), pltpu.SemaphoreType.DMA((168,)),
        ],
        compiler_params=pltpu.CompilerParams(
            collective_id=0, has_side_effects=True, vmem_limit_bytes=56 * 1024 * 1024
        ),
        name="layer",
    )(
        seg_lengths, tokens[0], prefix_keys[0], prefix_values[0], w_qkv, w_out, qk_scale, attn_rate,
        w_up, w_gate, w_down, up_scale, gate_scale, mlp_rate,
    )
    return out[None]


def solution(mesh):
    in_specs = (
        P("grp", "tok", None), P("grp", None), P("grp", "tok", None), P("grp", "tok", None),
        P(), P(), P(), P(), P(None, "grp"), P(None, "grp"), P("grp", None), P("grp"), P("grp"), P(),
    )
    return jax.shard_map(body, mesh=mesh, in_specs=in_specs, out_specs=P("grp", "tok", None), check_vma=False)
```
